768 devices in a mesh: lat: 64 (over y, x, core), lon: 12 (over z).
Axes of the slice: x: 4, y: 8, z: 12, core: 2. Of those that a mesh axis runs over, the one named last changes fastest.
Arguments:
- control: float32 [1024, 32, 1536], P('lat', None, 'lon'), may hold values from -6 to 6
- background: float32 [1024, 32, 1536], P('lat', None, 'lon'), may hold values from -6 to 6
- lon_width: int32 [1024], P('lat'), may hold values from 2 to 16
- block_cells: int32 [4096, 12], P('lat', 'lon'), may hold values from 0 to 255, as said below
- block_owner: int32 [4096, 12], P('lat', 'lon'), may hold values from -1 to 63, as said below
- channel_count: int32 [2112, 12], P('lat', 'lon'), may hold values from 1 to 256
- radiance: bfloat16 [16384, 3168], P('lat', 'lon'), may hold values from -6 to 6
- in_weight: bfloat16 [32, 1024], replicated, may hold values from -1 to 1
- in_bias: float32 [1024], replicated, may hold values from -3 to 3
- mid_weight: bfloat16 [1024, 1024], replicated, may hold values from -0.1875 to 0.1875
- mid_bias: float32 [1024], replicated, may hold values from -3 to 3
- out_weight: bfloat16 [1024, 256], replicated, may hold values from -0.1875 to 0.1875
- out_bias: float32 [256], replicated, may hold values from -3 to 3
Outputs:
- gradient: float32 [1024, 32, 1536], P('lat', None, 'lon')
The draws below stay inside these ranges and needn't reach their ends.
Inputs may be any that keep to these rules, and one draw needn't show every extreme that they name: `block_owner`: the live slots of a device come first, unused ones hold -1. Every device has at least 16 observed blocks, some device of every lon index has 64. One device sends at most 1 block to one owner, and an owner receives at most 33 blocks from its lon index; both bounds are reached in every draw. `block_cells`: the live slots of one device name distinct blocks.
All inputs are finite; a program needn't handle non-finite values.
Results may differ from the reference program's by a relative error of at most 0.0023.
Values may be sent and summed in bfloat16 or wider, within the bound.
A program may use at most 32 MiB of HBM per device.

```python
import jax
import jax.numpy as jnp
from jax import lax

LAT_DEV = 16
LON_DEV = 128
LEVELS = 32
NET_HIDDEN = 1024
CHANNELS = 256
REACH = 16
BLOCK_COLS = 8
OBS_MOST = 64
OBS_LOW = 32
RECV_MOST = 33
LAT_ROWS = 1024
LON_COLS = 1536
N_LAT = 64
N_LON = 12


def routing_tables(key):
    folded = jax.random.fold_in(key, 4711)
    key_count, key_busy, key_full, key_cells = jax.random.split(folded, 4)
    counts = jax.random.randint(key_count, (N_LAT, N_LON), OBS_LOW // 2, OBS_LOW + 1)
    busiest = jax.random.randint(key_busy, (N_LON,), 0, N_LAT)
    full_col = jax.random.randint(key_full, (), 0, N_LON)
    lat_ids = jnp.arange(N_LAT)[:, None]
    lon_ids = jnp.arange(N_LON)[None, :]
    counts = jnp.where(lon_ids == full_col, OBS_LOW, counts)
    counts = jnp.where(lat_ids == busiest[None, :], OBS_MOST, counts)
    starts = jnp.cumsum(counts, axis=0) - counts
    slot_ids = jnp.arange(OBS_MOST)[None, :, None]
    owners = jnp.where(slot_ids < counts[:, None, :], (starts[:, None, :] + slot_ids) % N_LAT, -1)
    cell_keys = jax.random.split(key_cells, N_LAT * N_LON)
    cell_total = LAT_DEV * (LON_DEV // BLOCK_COLS)
    shuffled = jax.vmap(lambda cell_key: jax.random.permutation(cell_key, cell_total)[:OBS_MOST])(cell_keys)
    cell_ids = jnp.transpose(shuffled.reshape(N_LAT, N_LON, OBS_MOST), (0, 2, 1))
    return (cell_ids.reshape(N_LAT * OBS_MOST, N_LON).astype(jnp.int32), owners.reshape(N_LAT * OBS_MOST, N_LON).astype(jnp.int32))


def draw_block_cells(key, part):
    return routing_tables(key)[0]


def draw_block_owner(key, part):
    return routing_tables(key)[1]


def place_ends(drawn, rng, smallest, largest):
    spot = [jax.random.randint(jax.random.fold_in(rng, axis), (), 0, length) for axis, length in enumerate(drawn.shape)]
    main_axis = drawn.shape.index(max(drawn.shape))
    beside = spot[:main_axis] + [(spot[main_axis] + 1) % drawn.shape[main_axis]] + spot[main_axis + 1:]
    return drawn.at[tuple(spot)].set(smallest).at[tuple(beside)].set(largest)


def levels(stream_key, dims, cuts, least, largest):
    gain, own = 1.0, jax.random.fold_in(stream_key, 6)
    for dim, parts in cuts:
        steps = jnp.exp(jax.random.uniform(jax.random.fold_in(own, dim), (parts,), jnp.float32, least / len(cuts), largest / len(cuts)))
        gain = gain * jnp.repeat(steps, dims[dim] // parts).reshape([-1 if axis == dim else 1 for axis in range(len(dims))])
    return gain


def bell_draw(own_key, shape, deviation, bound, pieces=(), kind=jnp.bfloat16):
    level = levels(own_key, shape, pieces, -0.22, 0.18) if pieces else 1.0
    values = jax.random.normal(own_key, shape, jnp.float32) * deviation * level
    return jnp.minimum(jnp.maximum(values, -bound), bound).astype(kind)


def setup_inputs(seed: int = 0) -> dict:
    streams_of = jax.random.split(jax.random.key(seed), 14)
    return {
        "control": bell_draw(streams_of[0], (LAT_ROWS, LEVELS, LON_COLS), 1.0, 6.0, ((0, 64), (2, 12)), jnp.float32),
        "background": bell_draw(streams_of[1], (LAT_ROWS, LEVELS, LON_COLS), 1.0, 6.0, ((0, 64), (2, 12)), jnp.float32),
        "lon_width": place_ends(jax.random.randint(streams_of[2], (LAT_ROWS,), 2, 17), jax.random.fold_in(streams_of[2], 1), 2, 16).astype(jnp.int32),
        "block_cells": draw_block_cells(jax.random.fold_in(streams_of[13], 71), 0),
        "block_owner": draw_block_owner(jax.random.fold_in(streams_of[13], 71), 0),
        "channel_count": place_ends(jax.random.randint(streams_of[5], (RECV_MOST * N_LAT, N_LON), 1, CHANNELS + 1), jax.random.fold_in(streams_of[5], 1), 1, CHANNELS).astype(jnp.int32),
        "radiance": bell_draw(streams_of[6], (N_LAT * CHANNELS, N_LON * RECV_MOST * BLOCK_COLS), 1.0, 6.0, ((0, 64), (1, 12))),
        "in_weight": bell_draw(streams_of[7], (LEVELS, NET_HIDDEN), LEVELS ** -0.5, 1.0),
        "in_bias": bell_draw(streams_of[8], (NET_HIDDEN,), 0.5, 3.0, (), jnp.float32),
        "mid_weight": bell_draw(streams_of[9], (NET_HIDDEN, NET_HIDDEN), NET_HIDDEN ** -0.5, 0.1875),
        "mid_bias": bell_draw(streams_of[10], (NET_HIDDEN,), 0.5, 3.0, (), jnp.float32),
        "out_weight": bell_draw(streams_of[11], (NET_HIDDEN, CHANNELS), NET_HIDDEN ** -0.5, 0.1875),
        "out_bias": bell_draw(streams_of[12], (CHANNELS,), 0.5, 3.0, (), jnp.float32),
    }


lat_sigma = 8.0

def tap_offsets():
    return jnp.arange(-REACH, REACH + 1).astype(jnp.float32)

def lat_taps():
    offsets = tap_offsets()
    raw_taps = jnp.exp(-offsets * offsets / (2.0 * lat_sigma * lat_sigma))
    return raw_taps / jnp.sqrt(jnp.sum(raw_taps * raw_taps))

def lon_taps(lon_width):
    offsets = tap_offsets()[None, :]
    spread = lon_width.astype(jnp.float32)[:, None]
    raw_taps = jnp.exp(-offsets * offsets / (2.0 * spread * spread))
    return raw_taps / jnp.sqrt(lax.optimization_barrier(jnp.sum(raw_taps * raw_taps, axis=1, keepdims=True)))

def smooth_lat(values):
    weights = lat_taps()
    padded = jnp.pad(values, ((REACH, REACH), (0, 0)))
    height = values.shape[0]
    summed = jnp.zeros_like(values)
    for offset in range(2 * REACH + 1):
        summed = summed + weights[offset] * padded[offset:offset + height]
    return summed

def smooth_lon(values, weights):
    summed = jnp.zeros_like(values)
    for offset in range(2 * REACH + 1):
        summed = summed + weights[:, offset][:, None] * jnp.roll(values, REACH - offset, axis=1)
    return summed

def per_level(values, plane_fn):

    def one_level(level):
        plane = lax.dynamic_index_in_dim(values, level, 1, keepdims=False)
        return plane_fn(plane)
    stacked = lax.map(one_level, jnp.arange(LEVELS).astype(jnp.int32))
    return jnp.transpose(stacked, (1, 0, 2))

def radiate(inputs, observed, kept_mask, in_weight, in_bias, mid_weight, mid_bias, out_weight, out_bias):
    first_pre = jnp.einsum('lh,lm->hm', in_weight.astype(jnp.float32), inputs.astype(jnp.float32)) + in_bias[:, None]
    act_one = lax.optimization_barrier(jnp.tanh(first_pre).astype(jnp.bfloat16))
    second_pre = jnp.einsum('hk,hm->km', mid_weight.astype(jnp.float32), act_one.astype(jnp.float32)) + mid_bias[:, None]
    act_two = lax.optimization_barrier(jnp.tanh(second_pre).astype(jnp.bfloat16))
    emitted = jnp.einsum('kn,km->nm', out_weight.astype(jnp.float32), act_two.astype(jnp.float32)) + out_bias[:, None]
    misfit = jnp.where(kept_mask, emitted - observed.astype(jnp.float32), 0.0)
    misfit = lax.optimization_barrier(misfit.astype(jnp.bfloat16))
    back_two = jnp.einsum('kn,nm->km', out_weight.astype(jnp.float32), misfit.astype(jnp.float32))
    two_val = act_two.astype(jnp.float32)
    grad_two = lax.optimization_barrier((back_two * (1.0 - two_val * two_val)).astype(jnp.bfloat16))
    back_one = jnp.einsum('hk,km->hm', mid_weight.astype(jnp.float32), grad_two.astype(jnp.float32))
    one_val = act_one.astype(jnp.float32)
    grad_one = lax.optimization_barrier((back_one * (1.0 - one_val * one_val)).astype(jnp.bfloat16))
    summed = jnp.einsum('lh,hm->lm', in_weight.astype(jnp.float32), grad_one.astype(jnp.float32))
    return lax.optimization_barrier(summed.astype(jnp.bfloat16))

def reference(control, background, lon_width, block_cells, block_owner, channel_count, radiance, in_weight, in_bias, mid_weight, mid_bias, out_weight, out_bias):
    lon_weights = lon_taps(lon_width)
    increment = per_level(control, lambda plane: smooth_lon(smooth_lat(plane), lon_weights))
    profile = lax.optimization_barrier((background + increment).astype(jnp.bfloat16))
    groups = LON_DEV // BLOCK_COLS
    entries = N_LAT * OBS_MOST
    slots_all = N_LAT * RECV_MOST
    entry_ids = jnp.arange(entries).astype(jnp.int32)
    slot_ids = jnp.arange(slots_all).astype(jnp.int32)
    channel_ids = jnp.arange(CHANNELS).astype(jnp.int32)

    def one_column(lon_index):
        owners = lax.dynamic_index_in_dim(block_owner, lon_index, 1, keepdims=False)
        picked_all = lax.dynamic_index_in_dim(block_cells, lon_index, 1, keepdims=False)
        counts = lax.dynamic_index_in_dim(channel_count, lon_index, 1, keepdims=False)
        start_col = (lon_index * LON_DEV).astype(jnp.int32)
        columns = lax.dynamic_slice_in_dim(profile, start_col, LON_DEV, 2)
        cells = columns.reshape(LAT_ROWS, LEVELS, groups, BLOCK_COLS)
        obs_start = (lon_index * RECV_MOST * BLOCK_COLS).astype(jnp.int32)
        observed = lax.dynamic_slice_in_dim(radiance, obs_start, RECV_MOST * BLOCK_COLS, 1)
        observed = jnp.transpose(observed.reshape(N_LAT, CHANNELS, RECV_MOST * BLOCK_COLS), (1, 0, 2)).reshape(CHANNELS, slots_all * BLOCK_COLS)
        is_live = owners >= 0
        same_owner = (owners[:, None] == owners[None, :]) & (entry_ids[None, :] < entry_ids[:, None])
        arrival = lax.optimization_barrier(jnp.sum(same_owner.astype(jnp.int32), axis=1)).astype(jnp.int32)
        target = jnp.where(is_live, owners * RECV_MOST + arrival, -1).astype(jnp.int32)
        matches = target[None, :] == slot_ids[:, None]
        filled = jnp.any(matches, axis=1)
        source = lax.optimization_barrier(jnp.sum(jnp.where(matches, entry_ids[None, :], 0), axis=1)).astype(jnp.int32)
        picked = picked_all[source]
        grid_row = (source // OBS_MOST * LAT_DEV + picked // groups).astype(jnp.int32)
        group = (picked % groups).astype(jnp.int32)
        blocks = cells[grid_row, :, group, :]
        blocks = jnp.where(filled[:, None, None], blocks, jnp.zeros((), jnp.bfloat16))
        inputs = jnp.transpose(blocks, (1, 0, 2)).reshape(LEVELS, slots_all * BLOCK_COLS)
        col_counts = jnp.broadcast_to(counts[:, None], (slots_all, BLOCK_COLS)).reshape(-1)
        col_filled = jnp.broadcast_to(filled[:, None], (slots_all, BLOCK_COLS)).reshape(-1)
        kept_mask = (channel_ids[:, None] < col_counts[None, :]) & col_filled[None, :]
        sensitivity = radiate(inputs, observed, kept_mask, in_weight, in_bias, mid_weight, mid_bias, out_weight, out_bias)
        sens_blocks = jnp.transpose(sensitivity.reshape(LEVELS, slots_all, BLOCK_COLS), (1, 0, 2)).astype(jnp.float32)
        landing = jnp.zeros((LAT_ROWS, LEVELS, groups, BLOCK_COLS), jnp.float32)
        drop_row = jnp.where(filled, grid_row, LAT_ROWS).astype(jnp.int32)
        landing = landing.at[drop_row, :, group, :].add(sens_blocks, mode='drop')
        return landing.reshape(LAT_ROWS, LEVELS, LON_DEV)
    landed = lax.map(one_column, jnp.arange(N_LON).astype(jnp.int32))
    landing = jnp.transpose(landed, (1, 2, 0, 3)).reshape(LAT_ROWS, LEVELS, LON_COLS)
    return control + per_level(landing, lambda plane: smooth_lat(smooth_lon(plane, lon_weights)))
```

```python
import functools

import jax
import jax.numpy as jnp
import numpy as np
from jax import lax
from jax.experimental import pallas as pl
from jax.experimental.pallas import tpu as pltpu
from jax.sharding import PartitionSpec as P

REACH = 16
BLOCK_COLS = 8
LAT_SIGMA = 8.0
UNSEEN = 32768.0
MESH = pl.DeviceIdType.MESH
F32 = jnp.float32
BF16 = jnp.bfloat16
I32 = jnp.int32
NN = (((1,), (0,)), ((), ()))
NT = (((1,), (1,)), ((), ()))

steps = np.arange(-REACH, REACH + 1).astype(np.float64)
raw = np.exp(-steps * steps / (2.0 * LAT_SIGMA**2))
LAT_TAPS = [float(v) for v in raw / np.sqrt(np.sum(raw * raw))]
LAT_NORM = float(1.0 / np.sqrt(np.sum(raw * raw)))


def dot(a, b, dims=NN):
    return lax.dot_general(a, b, dims, preferred_element_type=F32)


def split_two(value):
    high = value.astype(BF16)
    return high, (value - high.astype(F32)).astype(BF16)


def iota(shape, dim):
    return lax.broadcasted_iota(I32, shape, dim)


def smooth_rows(above, here, below, keep_above, keep_below, height, levels, store):
    def tile(t, carry):
        at = pl.ds(pl.multiple_of(t * 8, 8), 8)
        rows = [above[r, at, :] * keep_above for r in range(height)]
        rows += [here[r, at, :] for r in range(height)]
        rows += [below[r, at, :] * keep_below for r in range(height)]
        for r in range(height):
            total = rows[r + REACH] * LAT_TAPS[REACH]
            for j in range(1, REACH + 1):
                total += (rows[r + REACH - j] + rows[r + REACH + j]) * LAT_TAPS[REACH + j]
            store(r, at, total)
        return carry

    lax.fori_loop(0, levels // 8, tile, 0)


def kernel(
    n_lat,
    n_lon,
    control_hbm,
    background_hbm,
    width_ref,
    cells_ref,
    owner_ref,
    count_ref,
    radiance_hbm,
    w1_hbm,
    b1_ref,
    w2_hbm,
    b2_ref,
    w3_hbm,
    b3_ref,
    out_ref,
    control,
    background,
    radiance,
    w1,
    w2,
    w3,
    above,
    below,
    pack,
    from_left,
    from_right,
    flags,
    outgoing,
    observed,
    smooth,
    split_rows,
    split_back,
    rims,
    taps_high,
    taps_low,
    picks,
    band_high,
    band_low,
    back_rows,
    slot_rows,
    act_one,
    act_two,
    grad_two,
    grad_one,
    emitted,
    landed,
    landed_send,
    rim_send,
    above_back,
    below_back,
    left_back,
    right_back,
    local_sem,
    flag_send,
    flag_recv,
    rad_send,
    rad_recv,
    halo_send,
    halo_recv,
    back_send,
    back_recv,
):
    height, levels, width = control.shape
    slots = n_lat * BLOCK_COLS
    main = height * width
    side = height * REACH
    me = lax.axis_index("lat")
    col = lax.axis_index("lon")
    lat_at = {d: lax.rem(me + d + n_lat, n_lat) for d in (-1, 0, 1)}
    lon_at = {d: lax.rem(col + d + n_lon, n_lon) for d in (-1, 1)}

    barrier = pltpu.get_barrier_semaphore()
    for dl in (-1, 0, 1):
        for dq in (-1, 1):
            pl.semaphore_signal(
                barrier, inc=1, device_id=(lat_at[dl], lon_at[dq]), device_id_type=MESH
            )

    def greet(d, carry):
        pl.semaphore_signal(
            barrier, inc=1, device_id=(lax.rem(me + d, n_lat), col), device_id_type=MESH
        )
        return carry

    lax.fori_loop(1, n_lat, greet, 0)

    loads = [
        pltpu.make_async_copy(source, target, local_sem.at[k])
        for k, (source, target) in enumerate(
            (
                (control_hbm, control),
                (background_hbm, background),
                (radiance_hbm, radiance),
                (w1_hbm, w1),
                (w2_hbm, w2),
                (w3_hbm, w3),
            )
        )
    ]
    for load in loads:
        load.start()

    n_slots = owner_ref.shape[1]
    diag = iota((n_slots, n_slots), 0) == iota((n_slots, n_slots), 1)

    def upright(row):
        return jnp.sum(jnp.where(diag, row, 0), axis=1, keepdims=True)

    owner_col = upright(owner_ref[...])
    cells_col = upright(cells_ref[...])
    flags[pl.ds(me, 1)] = jnp.sum(
        (owner_col == iota((n_slots, 128), 1)).astype(F32), axis=0, keepdims=True
    ).reshape(1, 1, 128)

    loads[0].wait()
    lane = iota((levels, width), 1)
    per = width // REACH
    for k, start in enumerate((0, width - REACH)):
        for group in range(height // per):
            packed = jnp.zeros((levels, width), F32)
            for r in range(per):
                shift = (r * REACH - start) % width
                value = control[group * per + r]
                value = pltpu.roll(value, shift, 1) if shift else value
                packed = jnp.where(lane // REACH == r, value, packed)
            pack[k, group] = packed

    pl.semaphore_wait(barrier, n_lat - 1 + 6)

    def rim_copies(main_src, above_dst, below_dst, left_src, right_src, left_dst, right_dst, send, recv):
        copies = [
            pltpu.make_async_remote_copy(
                main_src, below_dst, send.at[0], recv.at[0], (lat_at[-1], col), MESH
            ),
            pltpu.make_async_remote_copy(
                main_src, above_dst, send.at[1], recv.at[1], (lat_at[1], col), MESH
            ),
        ]
        for dl in (-1, 0, 1):
            k = 2 + dl + 1
            copies.append(
                pltpu.make_async_remote_copy(
                    left_src, right_dst.at[1 - dl], send.at[k], recv.at[k],
                    (lat_at[dl], lon_at[-1]), MESH,
                )
            )
            copies.append(
                pltpu.make_async_remote_copy(
                    right_src, left_dst.at[1 - dl], send.at[k + 3], recv.at[k + 3],
                    (lat_at[dl], lon_at[1]), MESH,
                )
            )
        return copies

    def flag_copy(d):
        return pltpu.make_async_remote_copy(
            flags.at[me], flags.at[me], flag_send.at[d], flag_recv.at[d],
            (lax.rem(me + d, n_lat), col), MESH,
        )

    def rad_copy(d):
        target = lax.rem(me + d, n_lat)
        return pltpu.make_async_remote_copy(
            outgoing.at[target], observed.at[me], rad_send.at[d], rad_recv.at[d],
            (target, col), MESH,
        )

    def each(step):
        def body(d, carry):
            step(d)
            return carry

        lax.fori_loop(1, n_lat, body, 0)

    each(lambda d: flag_copy(d).start())
    halo = rim_copies(
        control, above, below, pack.at[0], pack.at[1], from_left, from_right, halo_send, halo_recv
    )
    for copy in halo:
        copy.start()

    mine = owner_col == iota((n_slots, slots), 1) // BLOCK_COLS
    cell = jnp.sum(jnp.where(mine, cells_col, 0), axis=0, keepdims=True)
    live = jnp.sum(mine.astype(F32), axis=0, keepdims=True)
    groups = width // BLOCK_COLS
    row_of = cell // groups
    lane_x = iota((1, slots), 1)
    place = (cell - row_of * groups) * BLOCK_COLS + lane_x % BLOCK_COLS
    spread = jnp.zeros((1, slots), F32)
    for r in range(height):
        spread += jnp.where(row_of == r, width_ref[r].astype(F32), 0.0)
    offset = iota((40, slots), 0).astype(F32) - REACH
    squares = jnp.sum(
        jnp.where(offset <= REACH, jnp.exp(-offset * offset / (spread * spread)), 0.0),
        axis=0,
        keepdims=True,
    )
    scale = live / jnp.sqrt(squares)
    rate = -0.5 / (spread * spread)

    def taps_at(column):
        away = (column - place).astype(F32)
        return jnp.where(jnp.abs(away) <= REACH, jnp.exp(away * away * rate) * scale, 0.0)

    column = iota((width, slots), 0)
    tap_high, tap_low = split_two(taps_at(column))
    pick = jnp.where(column == place, live, 0.0).astype(BF16)

    def lay(r, carry):
        rows = pl.ds(pl.multiple_of(r * width, width), width)
        keep = jnp.where(row_of == r, 1.0, 0.0).astype(BF16)
        taps_high[rows, :] = tap_high * keep
        taps_low[rows, :] = tap_low * keep
        picks[rows, :] = pick * keep
        return carry

    lax.fori_loop(0, height, lay, 0)
    rim = iota((side, slots), 0)
    for k, start in enumerate((-REACH, width)):
        value = jnp.where(rim // REACH == row_of, taps_at(rim % REACH + start), 0.0)
        high, low = split_two(value)
        taps_high[pl.ds(main + k * side, side), :] = high
        taps_low[pl.ds(main + k * side, side), :] = low

    rim_in = iota((3 * side, side), 0)
    rim_out = iota((3 * side, side), 1)
    away = (rim_in // REACH - height - rim_out // REACH).astype(F32)
    band = jnp.exp(away * away * (-0.5 / LAT_SIGMA**2)) * LAT_NORM
    band = jnp.where((jnp.abs(away) <= REACH) & (rim_in % REACH == rim_out % REACH), band, 0.0)
    high, low = split_two(band)
    band_high[...] = high
    band_low[...] = low

    loads[1].wait()
    for r in range(height):
        value = background[r]
        high, rest = split_two(value)
        middle = rest
        low = (value - high.astype(F32) - middle.astype(F32)).astype(BF16)
        lanes = pl.ds(r * width, width)
        split_back[pl.ds(0, levels), lanes] = high
        split_back[pl.ds(levels, levels), lanes] = middle
        split_back[pl.ds(2 * levels, levels), lanes] = low
    gathered = dot(split_back[...], picks[...])
    back_rows[...] = (
        gathered[:levels] + gathered[levels : 2 * levels] + gathered[2 * levels :]
    )

    loads[2].wait()
    n_recv = radiance.shape[0] // BLOCK_COLS
    channels = radiance.shape[1]
    counts = jnp.sum(
        jnp.where(
            iota((n_recv * BLOCK_COLS, n_recv), 1)
            == iota((n_recv * BLOCK_COLS, n_recv), 0) // BLOCK_COLS,
            count_ref[...],
            0,
        ),
        axis=1,
        keepdims=True,
    )
    seen = jnp.where(
        iota((n_recv * BLOCK_COLS, channels), 1) < counts, radiance[...].astype(F32), UNSEEN
    ).astype(BF16)

    each(lambda d: flag_copy(d).wait_recv())
    table = flags[...].reshape(n_lat, 128)
    sent = jnp.sum(
        jnp.where(iota((n_lat, 128), 1) == me, table, 0.0), axis=1, keepdims=True
    )
    sent = jnp.broadcast_to(sent, (n_lat, n_recv * BLOCK_COLS)).astype(BF16)
    source = iota((slots, n_lat), 0) // BLOCK_COLS
    entry = iota((slots, n_lat), 1)
    present = dot((entry == source).astype(BF16), sent)
    arrival = dot((entry < source).astype(BF16), sent)
    slot_x = iota((slots, n_recv * BLOCK_COLS), 1)
    row_x = iota((slots, n_recv * BLOCK_COLS), 0)
    select = (
        (present > 0.5)
        & (arrival == (slot_x // BLOCK_COLS).astype(F32))
        & (slot_x % BLOCK_COLS == row_x % BLOCK_COLS)
    )
    outgoing[...] = (
        dot(select.astype(BF16), seen).reshape(n_lat, BLOCK_COLS, channels).astype(BF16)
    )
    own = pltpu.make_async_copy(outgoing.at[me], observed.at[me], local_sem.at[6])
    own.start()
    each(lambda d: rad_copy(d).start())

    keep_above = jnp.where(me > 0, 1.0, 0.0).astype(F32)
    keep_below = jnp.where(me < n_lat - 1, 1.0, 0.0).astype(F32)
    for copy in halo:
        copy.wait_recv()

    def keep_smooth(r, at, value):
        smooth[r, at, :] = value

    smooth_rows(above, control, below, keep_above, keep_below, height, levels, keep_smooth)
    for r in range(height):
        high, low = split_two(smooth[r])
        split_rows[pl.ds(0, levels), pl.ds(r * width, width)] = high
        split_rows[pl.ds(levels, levels), pl.ds(r * width, width)] = low
    keeps = (keep_above, 1.0, keep_below)
    for k, ref in enumerate((from_left, from_right)):
        for b in range(3):
            for g in range(side // width):
                high, low = split_two(ref[b, g] * keeps[b])
                lanes = pl.ds(b * side + g * width, width)
                rims[pl.ds(k * levels, levels), lanes] = high
                rims[pl.ds((2 + k) * levels, levels), lanes] = low
    crossed = dot(rims[...], band_high[...])
    crossed = (
        crossed[: 2 * levels]
        + crossed[2 * levels :]
        + dot(rims[pl.ds(0, 2 * levels), :], band_low[...])
    )
    for k in range(2):
        high, low = split_two(crossed[k * levels : (k + 1) * levels])
        lanes = pl.ds(main + k * side, side)
        split_rows[pl.ds(0, levels), lanes] = high
        split_rows[pl.ds(levels, levels), lanes] = low
    total = dot(split_rows[...], taps_high[...])
    profile = (
        total[:levels]
        + total[levels:]
        + dot(split_rows[pl.ds(0, levels), :], taps_low[...])
        + back_rows[...]
    )
    slot_rows[...] = profile.T.astype(BF16)

    for load in loads[3:]:
        load.wait()
    tile = 256
    hidden = w2.shape[0]

    def lanes_of(n):
        return pl.ds(pl.multiple_of(n * tile, tile), tile)

    def first(n, carry):
        at = lanes_of(n)
        act_one[:, at] = jnp.tanh(dot(slot_rows[...], w1[:, at]) + b1_ref[:, at]).astype(BF16)
        return carry

    def second(n, carry):
        at = lanes_of(n)
        act_two[:, at] = jnp.tanh(dot(act_one[...], w2[:, at]) + b2_ref[:, at]).astype(BF16)
        return carry

    lax.fori_loop(0, hidden // tile, first, 0)
    lax.fori_loop(0, hidden // tile, second, 0)
    emitted[...] = dot(act_two[...], w3[...]) + b3_ref[...]

    own.wait()
    each(lambda d: rad_copy(d).wait_recv())
    target = observed[...].astype(F32).reshape(slots, channels)
    misfit = jnp.where(target < 0.5 * UNSEEN, emitted[...] - target, 0.0).astype(BF16)

    def second_back(n, carry):
        at = lanes_of(n)
        value = act_two[:, at].astype(F32)
        grad_two[:, at] = (dot(misfit, w3[at, :], NT) * (1.0 - value * value)).astype(BF16)
        return carry

    def first_back(n, carry):
        at = lanes_of(n)
        value = act_one[:, at].astype(F32)
        grad_one[:, at] = (dot(grad_two[...], w2[at, :], NT) * (1.0 - value * value)).astype(BF16)
        return carry

    lax.fori_loop(0, hidden // tile, second_back, 0)
    lax.fori_loop(0, hidden // tile, first_back, 0)
    sensitivity = dot(w1[...], grad_one[...], NT).astype(BF16)

    spreadout = dot(sensitivity, taps_high[...], NT)
    for r in range(height):
        value = spreadout[:, r * width : (r + 1) * width]
        landed[r] = value
        landed_send[r] = value.astype(BF16)
    for k in range(2):
        rim_send[k] = spreadout[:, main + k * side : main + (k + 1) * side].astype(BF16)
    back = rim_copies(
        landed_send, above_back, below_back, rim_send.at[0], rim_send.at[1],
        left_back, right_back, back_send, back_recv,
    )
    for copy in back:
        copy.start()
    for copy in back:
        copy.wait_recv()

    for r in range(height):
        above[r] = above_back[r].astype(F32)
        below[r] = below_back[r].astype(F32)
    for k, ref in enumerate((left_back, right_back)):
        for b in range(3):
            rims[pl.ds(k * levels, levels), pl.ds(b * side, side)] = (
                ref[b].astype(F32) * keeps[b]
            ).astype(BF16)
    crossed = dot(rims[pl.ds(0, 2 * levels), :], band_high[...])
    for r in range(height):
        at = slice(r // per * width, (r // per + 1) * width)
        value = control[r]
        low_cols = crossed[:levels, at]
        high_cols = crossed[levels:, at]
        shift = (-(r % per) * REACH) % width
        low_cols = pltpu.roll(low_cols, shift, 1) if shift else low_cols
        shift = (width - REACH - (r % per) * REACH) % width
        high_cols = pltpu.roll(high_cols, shift, 1) if shift else high_cols
        value += jnp.where(lane < REACH, low_cols, 0.0)
        value += jnp.where(lane >= width - REACH, high_cols, 0.0)
        smooth[r] = value

    def finish(r, at, value):
        out_ref[r, at, :] = smooth[r, at, :] + value

    smooth_rows(above, landed, below, keep_above, keep_below, height, levels, finish)

    each(lambda d: flag_copy(d).wait_send())
    each(lambda d: rad_copy(d).wait_send())
    for copy in halo + back:
        copy.wait_send()


def shards(
    n_lat,
    n_lon,
    control,
    background,
    lon_width,
    block_cells,
    block_owner,
    channel_count,
    radiance,
    in_weight,
    in_bias,
    mid_weight,
    mid_bias,
    out_weight,
    out_bias,
):
    height, levels, width = control.shape
    hidden = mid_weight.shape[0]
    channels, recv_cols = radiance.shape
    slots = n_lat * BLOCK_COLS
    main = height * width
    side = height * REACH
    per_side = side // width
    dma = pltpu.SemaphoreType.DMA
    vmem = pltpu.VMEM
    any_spec = pl.BlockSpec(memory_space=pl.ANY)
    vmem_spec = pl.BlockSpec(memory_space=pltpu.VMEM)
    smem_spec = pl.BlockSpec(memory_space=pltpu.SMEM)
    grid = (height, levels, width)
    return pl.pallas_call(
        functools.partial(kernel, n_lat, n_lon),
        out_shape=jax.ShapeDtypeStruct(grid, F32),
        in_specs=[
            any_spec, any_spec, smem_spec, vmem_spec, vmem_spec, vmem_spec, any_spec,
            any_spec, vmem_spec, any_spec, vmem_spec, any_spec, vmem_spec,
        ],
        out_specs=vmem_spec,
        scratch_shapes=[
            vmem(grid, F32),
            vmem(grid, F32),
            vmem((recv_cols, channels), BF16),
            vmem((levels, hidden), BF16),
            vmem((hidden, hidden), BF16),
            vmem((hidden, channels), BF16),
            vmem(grid, F32),
            vmem(grid, F32),
            vmem((2, per_side, levels, width), F32),
            vmem((3, per_side, levels, width), F32),
            vmem((3, per_side, levels, width), F32),
            vmem((n_lat, 1, 128), F32),
            vmem((n_lat, BLOCK_COLS, channels), BF16),
            vmem((n_lat, BLOCK_COLS, channels), BF16),
            vmem(grid, F32),
            vmem((2 * levels, main + 2 * side), BF16),
            vmem((3 * levels, main), BF16),
            vmem((4 * levels, 3 * side), BF16),
            vmem((main + 2 * side, slots), BF16),
            vmem((main + 2 * side, slots), BF16),
            vmem((main, slots), BF16),
            vmem((3 * side, side), BF16),
            vmem((3 * side, side), BF16),
            vmem((levels, slots), F32),
            vmem((slots, levels), BF16),
            vmem((slots, hidden), BF16),
            vmem((slots, hidden), BF16),
            vmem((slots, hidden), BF16),
            vmem((slots, hidden), BF16),
            vmem((slots, channels), F32),
            vmem(grid, F32),
            vmem(grid, BF16),
            vmem((2, levels, side), BF16),
            vmem(grid, BF16),
            vmem(grid, BF16),
            vmem((3, levels, side), BF16),
            vmem((3, levels, side), BF16),
            dma((8,)),
            dma((n_lat,)),
            dma((n_lat,)),
            dma((n_lat,)),
            dma((n_lat,)),
            dma((8,)),
            dma((8,)),
            dma((8,)),
            dma((8,)),
        ],
        compiler_params=pltpu.CompilerParams(
            collective_id=0, has_side_effects=True, vmem_limit_bytes=60 * 1024 * 1024
        ),
    )(
        control,
        background,
        lon_width,
        block_cells.T,
        block_owner.T,
        channel_count.T,
        radiance.T,
        in_weight,
        in_bias.reshape(1, -1),
        mid_weight,
        mid_bias.reshape(1, -1),
        out_weight,
        out_bias.reshape(1, -1),
    )


def solution(mesh):
    return jax.shard_map(
        functools.partial(shards, mesh.shape["lat"], mesh.shape["lon"]),
        mesh=mesh,
        in_specs=(
            P("lat", None, "lon"),
            P("lat", None, "lon"),
            P("lat"),
            P("lat", "lon"),
            P("lat", "lon"),
            P("lat", "lon"),
            P("lat", "lon"),
            P(),
            P(),
            P(),
            P(),
            P(),
            P(),
        ),
        out_specs=P("lat", None, "lon"),
        check_vma=False,
    )
```

```python
import functools

import jax
import jax.numpy as jnp
import numpy as np
from jax import lax
from jax.experimental import pallas as pl
from jax.experimental.pallas import tpu as pltpu
from jax.sharding import PartitionSpec as P

REACH = 16
BLOCK_COLS = 8
LAT_SIGMA = 8.0
CHUNKS = 4
UNSEEN = 32768.0
MESH = pl.DeviceIdType.MESH
F32 = jnp.float32
BF16 = jnp.bfloat16
I32 = jnp.int32
NN = (((1,), (0,)), ((), ()))
NT = (((1,), (1,)), ((), ()))

steps = np.arange(-REACH, REACH + 1).astype(np.float64)
raw = np.exp(-steps * steps / (2.0 * LAT_SIGMA**2))
LAT_TAPS = [float(v) for v in raw / np.sqrt(np.sum(raw * raw))]
LAT_NORM = float(1.0 / np.sqrt(np.sum(raw * raw)))


def dot(a, b, dims=NN):
    return lax.dot_general(a, b, dims, preferred_element_type=F32)


def split_two(value):
    high = value.astype(BF16)
    return high, (value - high.astype(F32)).astype(BF16)


def iota(shape, dim):
    return lax.broadcasted_iota(I32, shape, dim)


def by_distance(count):
    return sorted(range(count), key=lambda d: (min(d, count - d), d))


def choose(index, values):
    chosen = jnp.zeros_like(index)
    for k, value in enumerate(values):
        chosen = jnp.where(index == k, value, chosen)
    return chosen


def smooth_rows(above, here, below, keep_above, keep_below, height, levels, store):
    def tile(t, carry):
        at = pl.ds(pl.multiple_of(t * 8, 8), 8)
        rows = [above[r, at, :] * keep_above for r in range(height)]
        rows += [here[r, at, :] for r in range(height)]
        rows += [below[r, at, :] * keep_below for r in range(height)]
        for r in range(height):
            total = rows[r + REACH] * LAT_TAPS[REACH]
            for j in range(1, REACH + 1):
                total += (rows[r + REACH - j] + rows[r + REACH + j]) * LAT_TAPS[REACH + j]
            store(r, at, total)
        return carry

    lax.fori_loop(0, levels // 8, tile, 0, unroll=True)


def kernel(
    n_lat,
    n_lon,
    control_hbm,
    background_hbm,
    width_hbm,
    cells_hbm,
    owner_hbm,
    count_hbm,
    radiance_hbm,
    w1_hbm,
    b1_hbm,
    w2_hbm,
    b2_hbm,
    w3_hbm,
    b3_hbm,
    out_ref,
    width_ref,
    cells_ref,
    owner_ref,
    count_ref,
    b1_ref,
    b2_ref,
    b3_ref,
    control,
    background,
    radiance,
    w1,
    w2,
    w3,
    above,
    below,
    pack,
    from_left,
    from_right,
    flags,
    outgoing,
    observed,
    smooth,
    split_rows,
    split_back,
    rims,
    taps_high,
    taps_low,
    picks,
    band_high,
    band_low,
    back_rows,
    slot_rows,
    act_one,
    act_two,
    grad_two,
    grad_one,
    emitted,
    misfit,
    landed,
    landed_send,
    rim_send,
    above_back,
    below_back,
    left_back,
    right_back,
    local_sem,
    flag_send,
    flag_recv,
    rad_send,
    rad_recv,
    halo_send,
    halo_recv,
    back_send,
    back_recv,
):
    height, levels, width = control.shape
    slots = n_lat * BLOCK_COLS
    main = height * width
    side = height * REACH
    me = lax.axis_index("lat")
    col = lax.axis_index("lon")
    lat_at = {d: lax.rem(me + d + n_lat, n_lat) for d in (-1, 0, 1)}
    lon_at = {d: lax.rem(col + d + n_lon, n_lon) for d in (-1, 1)}

    n_row = 8 if n_lat % 16 == 0 else 2
    n_far = n_lat // n_row
    far = me // n_row
    near = me - far * n_row
    rings = by_distance(n_far)
    reaches = [(df, dn) for df in rings[::-1] for dn in range(n_row) if df or dn]

    def peer(df, dn):
        return lax.rem(far + df, n_far) * n_row + lax.rem(near + dn, n_row)

    barrier = pltpu.get_barrier_semaphore()
    for df, dn in reaches:
        pl.semaphore_signal(barrier, inc=1, device_id=(peer(df, dn), col), device_id_type=MESH)
    for dl in (-1, 0, 1):
        for dq in (-1, 1):
            pl.semaphore_signal(
                barrier, inc=1, device_id=(lat_at[dl], lon_at[dq]), device_id_type=MESH
            )

    loads = [
        pltpu.make_async_copy(source, target, local_sem.at[k])
        for k, (source, target) in enumerate(
            (
                (owner_hbm, owner_ref),
                (cells_hbm, cells_ref),
                (width_hbm, width_ref),
                (control_hbm, control),
                (background_hbm, background),
                (count_hbm, count_ref),
                (radiance_hbm, radiance),
                (w1_hbm, w1),
                (b1_hbm, b1_ref),
                (w2_hbm, w2),
                (b2_hbm, b2_ref),
                (w3_hbm, w3),
                (b3_hbm, b3_ref),
            )
        )
    ]
    for load in loads[:4]:
        load.start()

    n_slots = owner_ref.shape[1]
    for load in loads[:3]:
        load.wait()
    diag = iota((n_slots, n_slots), 0) == iota((n_slots, n_slots), 1)

    def upright(row):
        return jnp.sum(jnp.where(diag, row, 0), axis=1, keepdims=True)

    owner_col = upright(owner_ref[...])
    cells_col = upright(cells_ref[...])
    flags[pl.ds(me, 1)] = jnp.sum(
        (owner_col == iota((n_slots, 128), 1)).astype(F32), axis=0, keepdims=True
    ).reshape(1, 1, 128)

    loads[3].wait()
    lane = iota((levels, width), 1)
    per = width // REACH
    for k, start in enumerate((0, width - REACH)):
        for group in range(height // per):
            packed = jnp.zeros((levels, width), F32)
            for r in range(per):
                shift = (r * REACH - start) % width
                value = control[group * per + r]
                value = pltpu.roll(value, shift, 1) if shift else value
                packed = jnp.where(lane // REACH == r, value, packed)
            pack[k, group] = packed

    pl.semaphore_wait(barrier, n_lat - 1 + 6)

    def side_copies(left_src, right_src, left_dst, right_dst, send, recv):
        copies = []
        for dl in (-1, 0, 1):
            k = dl + 1
            copies.append(
                pltpu.make_async_remote_copy(
                    left_src, right_dst.at[1 - dl], send.at[k], recv.at[k],
                    (lat_at[dl], lon_at[-1]), MESH,
                )
            )
            copies.append(
                pltpu.make_async_remote_copy(
                    right_src, left_dst.at[1 - dl], send.at[k + 3], recv.at[k + 3],
                    (lat_at[dl], lon_at[1]), MESH,
                )
            )
        return copies

    def band_copies(source, above_dst, below_dst, send, recv, k):
        return [
            pltpu.make_async_remote_copy(
                source, below_dst, send.at[k], recv.at[k], (lat_at[-1], col), MESH
            ),
            pltpu.make_async_remote_copy(
                source, above_dst, send.at[k + 1], recv.at[k + 1], (lat_at[1], col), MESH
            ),
        ]

    flag_copies = [
        pltpu.make_async_remote_copy(
            flags.at[me], flags.at[me], flag_send.at[df * n_row + dn],
            flag_recv.at[df * n_row + dn], (peer(df, dn), col), MESH,
        )
        for df, dn in reaches
    ]

    def rad_copy(df, dn):
        source = rings[::-1].index(df) * n_row + lax.rem(near + dn, n_row)
        place = rings.index((n_far - df) % n_far) * n_row + near
        return pltpu.make_async_remote_copy(
            outgoing.at[source], observed.at[place], rad_send.at[df * n_row + dn],
            rad_recv.at[df * n_row + dn], (peer(df, dn), col), MESH,
        )

    for copy in flag_copies:
        copy.start()
    halo = band_copies(control, above, below, halo_send, halo_recv, 6)
    halo += side_copies(pack.at[0], pack.at[1], from_left, from_right, halo_send, halo_recv)
    for copy in halo:
        copy.start()
    for load in loads[4:]:
        load.start()

    lane_o = iota((1, slots), 1) // BLOCK_COLS
    owner_o = lax.rem(choose(lane_o // n_row, rings) + far, n_far) * n_row + lane_o % n_row
    mine = owner_col == owner_o
    cell = jnp.sum(jnp.where(mine, cells_col, 0), axis=0, keepdims=True)
    live = jnp.sum(mine.astype(F32), axis=0, keepdims=True)
    groups = width // BLOCK_COLS
    row_of = cell // groups
    lane_x = iota((1, slots), 1)
    place = (cell - row_of * groups) * BLOCK_COLS + lane_x % BLOCK_COLS
    spread = jnp.zeros((1, slots), F32)
    for r in range(height):
        spread += jnp.where(row_of == r, width_ref[r].astype(F32), 0.0)
    offset = iota((40, slots), 0).astype(F32) - REACH
    squares = jnp.sum(
        jnp.where(offset <= REACH, jnp.exp(-offset * offset / (spread * spread)), 0.0),
        axis=0,
        keepdims=True,
    )
    scale = live / jnp.sqrt(squares)
    rate = -0.5 / (spread * spread)

    def taps_at(column):
        away = (column - place).astype(F32)
        return jnp.where(jnp.abs(away) <= REACH, jnp.exp(away * away * rate) * scale, 0.0)

    column = iota((width, slots), 0)
    tap_high, tap_low = split_two(taps_at(column))
    pick = jnp.where(column == place, live, 0.0).astype(BF16)

    def lay(r, carry):
        rows = pl.ds(pl.multiple_of(r * width, width), width)
        keep = jnp.where(row_of == r, 1.0, 0.0).astype(BF16)
        taps_high[rows, :] = tap_high * keep
        taps_low[rows, :] = tap_low * keep
        picks[rows, :] = pick * keep
        return carry

    lax.fori_loop(0, height, lay, 0, unroll=True)
    rim = iota((side, slots), 0)
    for k, start in enumerate((-REACH, width)):
        value = jnp.where(rim // REACH == row_of, taps_at(rim % REACH + start), 0.0)
        high, low = split_two(value)
        taps_high[pl.ds(main + k * side, side), :] = high
        taps_low[pl.ds(main + k * side, side), :] = low

    rim_in = iota((3 * side, side), 0)
    rim_out = iota((3 * side, side), 1)
    away = (rim_in // REACH - height - rim_out // REACH).astype(F32)
    band = jnp.exp(away * away * (-0.5 / LAT_SIGMA**2)) * LAT_NORM
    band = jnp.where((jnp.abs(away) <= REACH) & (rim_in % REACH == rim_out % REACH), band, 0.0)
    high, low = split_two(band)
    band_high[...] = high
    band_low[...] = low

    loads[4].wait()
    for r in range(height):
        value = background[r]
        high, rest = split_two(value)
        middle = rest
        low = (value - high.astype(F32) - middle.astype(F32)).astype(BF16)
        lanes = pl.ds(r * width, width)
        split_back[pl.ds(0, levels), lanes] = high
        split_back[pl.ds(levels, levels), lanes] = middle
        split_back[pl.ds(2 * levels, levels), lanes] = low
    gathered = dot(split_back[...], picks[...])
    back_rows[...] = (
        gathered[:levels] + gathered[levels : 2 * levels] + gathered[2 * levels :]
    )

    for load in loads[5:7]:
        load.wait()
    n_recv = radiance.shape[0] // BLOCK_COLS
    channels = radiance.shape[1]
    counts = jnp.sum(
        jnp.where(
            iota((n_recv * BLOCK_COLS, n_recv), 1)
            == iota((n_recv * BLOCK_COLS, n_recv), 0) // BLOCK_COLS,
            count_ref[...],
            0,
        ),
        axis=1,
        keepdims=True,
    )
    seen = jnp.where(
        iota((n_recv * BLOCK_COLS, channels), 1) < counts, radiance[...].astype(F32), UNSEEN
    ).astype(BF16)

    for copy in flag_copies:
        copy.wait_recv()
    table = flags[...].reshape(n_lat, 128)
    sent = jnp.sum(
        jnp.where(iota((n_lat, 128), 1) == me, table, 0.0), axis=1, keepdims=True
    )
    sent = jnp.broadcast_to(sent, (n_lat, n_recv * BLOCK_COLS)).astype(BF16)
    half = slots // 2
    rads = {}
    for part in range(2):
        row_o = (iota((half, n_lat), 0) + part * half) // BLOCK_COLS
        source = lax.rem(choose(row_o // n_row, rings[::-1]) + far, n_far) * n_row + row_o % n_row
        entry = iota((half, n_lat), 1)
        present = dot((entry == source).astype(BF16), sent)
        arrival = dot((entry < source).astype(BF16), sent)
        slot_x = iota((half, n_recv * BLOCK_COLS), 1)
        row_x = iota((half, n_recv * BLOCK_COLS), 0)
        select = (
            (present > 0.5)
            & (arrival == (slot_x // BLOCK_COLS).astype(F32))
            & (slot_x % BLOCK_COLS == row_x % BLOCK_COLS)
        )
        outgoing[pl.ds(part * (n_lat // 2), n_lat // 2)] = (
            dot(select.astype(BF16), seen).reshape(n_lat // 2, BLOCK_COLS, channels).astype(BF16)
        )
        for df, dn in reaches:
            if rings[::-1].index(df) * 2 // n_far == part:
                rads[df, dn] = rad_copy(df, dn)
                rads[df, dn].start()
    own = pltpu.make_async_copy(
        outgoing.at[(n_far - 1) * n_row + near], observed.at[near], local_sem.at[len(loads)]
    )
    own.start()

    keep_above = jnp.where(me > 0, 1.0, 0.0).astype(F32)
    keep_below = jnp.where(me < n_lat - 1, 1.0, 0.0).astype(F32)
    for copy in halo:
        copy.wait_recv()

    def keep_smooth(r, at, value):
        smooth[r, at, :] = value

    smooth_rows(above, control, below, keep_above, keep_below, height, levels, keep_smooth)
    for r in range(height):
        high, low = split_two(smooth[r])
        split_rows[pl.ds(0, levels), pl.ds(r * width, width)] = high
        split_rows[pl.ds(levels, levels), pl.ds(r * width, width)] = low
    keeps = (keep_above, 1.0, keep_below)
    for k, ref in enumerate((from_left, from_right)):
        for b in range(3):
            for g in range(side // width):
                high, low = split_two(ref[b, g] * keeps[b])
                lanes = pl.ds(b * side + g * width, width)
                rims[pl.ds(k * levels, levels), lanes] = high
                rims[pl.ds((2 + k) * levels, levels), lanes] = low
    crossed = dot(rims[...], band_high[...])
    crossed = (
        crossed[: 2 * levels]
        + crossed[2 * levels :]
        + dot(rims[pl.ds(0, 2 * levels), :], band_low[...])
    )
    for k in range(2):
        high, low = split_two(crossed[k * levels : (k + 1) * levels])
        lanes = pl.ds(main + k * side, side)
        split_rows[pl.ds(0, levels), lanes] = high
        split_rows[pl.ds(levels, levels), lanes] = low
    total = dot(split_rows[...], taps_high[...])
    profile = (
        total[:levels]
        + total[levels:]
        + dot(split_rows[pl.ds(0, levels), :], taps_low[...])
        + back_rows[...]
    )
    slot_rows[...] = profile.T.astype(BF16)

    for load in loads[7:]:
        load.wait()
    tile = 256
    hidden = w2.shape[0]

    def lanes_of(n):
        return pl.ds(pl.multiple_of(n * tile, tile), tile)

    def first(n, carry):
        at = lanes_of(n)
        act_one[:, at] = jnp.tanh(dot(slot_rows[...], w1[:, at]) + b1_ref[:, at]).astype(BF16)
        return carry

    def second(n, carry):
        at = lanes_of(n)
        act_two[:, at] = jnp.tanh(dot(act_one[...], w2[:, at]) + b2_ref[:, at]).astype(BF16)
        return carry

    lax.fori_loop(0, hidden // tile, first, 0, unroll=True)
    lax.fori_loop(0, hidden // tile, second, 0, unroll=True)
    emitted[...] = dot(act_two[...], w3[...]) + b3_ref[...]

    own.wait()
    for part in range(2):
        for df, dn in reaches:
            if rings.index((n_far - df) % n_far) * 2 // n_far == part:
                rads[df, dn].wait_recv()
        rows = pl.ds(part * half, half)
        target = observed[pl.ds(part * (n_lat // 2), n_lat // 2)].astype(F32).reshape(half, channels)
        misfit[...] = jnp.where(
            target < 0.5 * UNSEEN, emitted[rows, :] - target, 0.0
        ).astype(BF16)

        def second_back(n, carry):
            at = lanes_of(n)
            value = act_two[rows, at].astype(F32)
            grad_two[:, at] = (dot(misfit[...], w3[at, :], NT) * (1.0 - value * value)).astype(BF16)
            return carry

        def first_back(n, carry):
            at = lanes_of(n)
            value = act_one[rows, at].astype(F32)
            grad_one[rows, at] = (
                dot(grad_two[...], w2[at, :], NT) * (1.0 - value * value)
            ).astype(BF16)
            return carry

        lax.fori_loop(0, hidden // tile, second_back, 0, unroll=True)
        lax.fori_loop(0, hidden // tile, first_back, 0, unroll=True)
    sensitivity = dot(w1[...], grad_one[...], NT).astype(BF16)

    edges = dot(sensitivity, taps_high[pl.ds(main, 2 * side), :], NT).astype(BF16)
    for k in range(2):
        rim_send[k] = edges[:, k * side : (k + 1) * side]
    sides = side_copies(
        rim_send.at[0], rim_send.at[1], left_back, right_back, back_send, back_recv
    )
    for copy in sides:
        copy.start()
    bands = []
    chunk = height // CHUNKS
    for part in range(CHUNKS):
        rows = pl.ds(part * chunk, chunk)
        spreadout = dot(sensitivity, taps_high[pl.ds(part * chunk * width, chunk * width), :], NT)
        for r in range(chunk):
            value = spreadout[:, r * width : (r + 1) * width]
            landed[part * chunk + r] = value
            landed_send[part * chunk + r] = value.astype(BF16)
        bands += band_copies(
            landed_send.at[rows], above_back.at[rows], below_back.at[rows],
            back_send, back_recv, 6 + 2 * part,
        )
        for copy in bands[-2:]:
            copy.start()

    def own_rows(t, carry):
        at = pl.ds(pl.multiple_of(t * 8, 8), 8)
        values = [landed[r, at, :] for r in range(height)]
        for r in range(height):
            total = values[r] * LAT_TAPS[REACH]
            for j in range(1, height):
                pair = [values[k] for k in (r - j, r + j) if 0 <= k < height]
                if pair:
                    total += sum(pair[1:], pair[0]) * LAT_TAPS[REACH + j]
            smooth[r, at, :] = total
        return carry

    lax.fori_loop(0, levels // 8, own_rows, 0, unroll=True)
    for copy in bands:
        copy.wait_recv()
    for r in range(height):
        above[r] = above_back[r].astype(F32) * keep_above
        below[r] = below_back[r].astype(F32) * keep_below

    def other_rows(t, carry):
        at = pl.ds(pl.multiple_of(t * 8, 8), 8)
        upper = [above[r, at, :] for r in range(height)]
        lower = [below[r, at, :] for r in range(height)]
        for r in range(height):
            total = smooth[r, at, :]
            for k in range(height):
                if r + height - k <= REACH:
                    total += upper[k] * LAT_TAPS[REACH + r + height - k]
                if k + height - r <= REACH:
                    total += lower[k] * LAT_TAPS[REACH + k + height - r]
            smooth[r, at, :] = total
        return carry

    lax.fori_loop(0, levels // 8, other_rows, 0, unroll=True)
    for copy in sides:
        copy.wait_recv()
    for k, ref in enumerate((left_back, right_back)):
        for b in range(3):
            rims[pl.ds(k * levels, levels), pl.ds(b * side, side)] = (
                ref[b].astype(F32) * keeps[b]
            ).astype(BF16)
    crossed = dot(rims[pl.ds(0, 2 * levels), :], band_high[...])
    for r in range(height):
        at = slice(r // per * width, (r // per + 1) * width)
        low_cols = crossed[:levels, at]
        high_cols = crossed[levels:, at]
        shift = (-(r % per) * REACH) % width
        low_cols = pltpu.roll(low_cols, shift, 1) if shift else low_cols
        shift = (width - REACH - (r % per) * REACH) % width
        high_cols = pltpu.roll(high_cols, shift, 1) if shift else high_cols
        edge = jnp.where(lane < REACH, low_cols, jnp.where(lane >= width - REACH, high_cols, 0.0))
        out_ref[r] = smooth[r] + edge

    for copy in flag_copies + list(rads.values()) + halo + sides + bands:
        copy.wait_send()


def shards(
    n_lat,
    n_lon,
    control,
    background,
    lon_width,
    block_cells,
    block_owner,
    channel_count,
    radiance,
    in_weight,
    in_bias,
    mid_weight,
    mid_bias,
    out_weight,
    out_bias,
):
    height, levels, width = control.shape
    hidden = mid_weight.shape[0]
    channels, recv_cols = radiance.shape
    slots = n_lat * BLOCK_COLS
    main = height * width
    side = height * REACH
    per_side = side // width
    dma = pltpu.SemaphoreType.DMA
    vmem = pltpu.VMEM
    hbm_spec = pl.BlockSpec(memory_space=pltpu.HBM)
    vmem_spec = pl.BlockSpec(memory_space=pltpu.VMEM)
    grid = (height, levels, width)
    adjoint = pl.pallas_call(
        functools.partial(kernel, n_lat, n_lon),
        out_shape=jax.ShapeDtypeStruct(grid, F32),
        in_specs=[hbm_spec] * 13,
        out_specs=vmem_spec,
        scratch_shapes=[
            pltpu.SMEM(lon_width.shape, I32),
            vmem((1, block_cells.shape[0]), I32),
            vmem((1, block_owner.shape[0]), I32),
            vmem((1, channel_count.shape[0]), I32),
            vmem((1, hidden), F32),
            vmem((1, hidden), F32),
            vmem((1, channels), F32),
            vmem(grid, F32),
            vmem(grid, F32),
            vmem((recv_cols, channels), BF16),
            vmem((levels, hidden), BF16),
            vmem((hidden, hidden), BF16),
            vmem((hidden, channels), BF16),
            vmem(grid, F32),
            vmem(grid, F32),
            vmem((2, per_side, levels, width), F32),
            vmem((3, per_side, levels, width), F32),
            vmem((3, per_side, levels, width), F32),
            vmem((n_lat, 1, 128), F32),
            vmem((n_lat, BLOCK_COLS, channels), BF16),
            vmem((n_lat, BLOCK_COLS, channels), BF16),
            vmem(grid, F32),
            vmem((2 * levels, main + 2 * side), BF16),
            vmem((3 * levels, main), BF16),
            vmem((4 * levels, 3 * side), BF16),
            vmem((main + 2 * side, slots), BF16),
            vmem((main + 2 * side, slots), BF16),
            vmem((main, slots), BF16),
            vmem((3 * side, side), BF16),
            vmem((3 * side, side), BF16),
            vmem((levels, slots), F32),
            vmem((slots, levels), BF16),
            vmem((slots, hidden), BF16),
            vmem((slots, hidden), BF16),
            vmem((slots // 2, hidden), BF16),
            vmem((slots, hidden), BF16),
            vmem((slots, channels), F32),
            vmem((slots // 2, channels), BF16),
            vmem(grid, F32),
            vmem(grid, BF16),
            vmem((2, levels, side), BF16),
            vmem(grid, BF16),
            vmem(grid, BF16),
            vmem((3, levels, side), BF16),
            vmem((3, levels, side), BF16),
            dma((14,)),
            dma((n_lat,)),
            dma((n_lat,)),
            dma((n_lat,)),
            dma((n_lat,)),
            dma((8,)),
            dma((8,)),
            dma((6 + 2 * CHUNKS,)),
            dma((6 + 2 * CHUNKS,)),
        ],
        compiler_params=pltpu.CompilerParams(
            collective_id=0, has_side_effects=True, vmem_limit_bytes=26 * 1024 * 1024
        ),
    )(
        *(
            pltpu.with_memory_space_constraint(value, pltpu.HBM)
            for value in (
                control,
                background,
                lon_width,
                block_cells.T,
                block_owner.T,
                channel_count.T,
                radiance.T,
                in_weight,
                in_bias.reshape(1, -1),
                mid_weight,
                mid_bias.reshape(1, -1),
                out_weight,
                out_bias.reshape(1, -1),
            )
        )
    )
    return control + adjoint


def solution(mesh):
    return jax.shard_map(
        functools.partial(shards, mesh.shape["lat"], mesh.shape["lon"]),
        mesh=mesh,
        in_specs=(
            P("lat", None, "lon"),
            P("lat", None, "lon"),
            P("lat"),
            P("lat", "lon"),
            P("lat", "lon"),
            P("lat", "lon"),
            P("lat", "lon"),
            P(),
            P(),
            P(),
            P(),
            P(),
            P(),
        ),
        out_specs=P("lat", None, "lon"),
        check_vma=False,
    )
```

```python
import functools

import jax
import jax.numpy as jnp
import numpy as np
from jax import lax
from jax.experimental import pallas as pl
from jax.experimental.pallas import tpu as pltpu
from jax.sharding import PartitionSpec as P

REACH = 16
BLOCK_COLS = 8
LAT_SIGMA = 8.0
CHUNKS = 4
SEND_PARTS = 2
BACK_PARTS = 1
UNSEEN = 32768.0
MESH = pl.DeviceIdType.MESH
F32 = jnp.float32
BF16 = jnp.bfloat16
I32 = jnp.int32
NN = (((1,), (0,)), ((), ()))
NT = (((1,), (1,)), ((), ()))

steps = np.arange(-REACH, REACH + 1).astype(np.float64)
raw = np.exp(-steps * steps / (2.0 * LAT_SIGMA**2))
LAT_TAPS = [float(v) for v in raw / np.sqrt(np.sum(raw * raw))]
LAT_NORM = float(1.0 / np.sqrt(np.sum(raw * raw)))


def dot(a, b, dims=NN):
    return lax.dot_general(a, b, dims, preferred_element_type=F32)


def split_two(value):
    high = value.astype(BF16)
    return high, (value - high.astype(F32)).astype(BF16)


def iota(shape, dim):
    return lax.broadcasted_iota(I32, shape, dim)


def by_distance(count):
    return sorted(range(count), key=lambda d: (min(d, count - d), d))


def choose(index, values):
    chosen = jnp.zeros_like(index)
    for k, value in enumerate(values):
        chosen = jnp.where(index == k, value, chosen)
    return chosen


def smooth_rows(above, here, below, keep_above, keep_below, height, levels, store):
    def tile(t, carry):
        at = pl.ds(pl.multiple_of(t * 8, 8), 8)
        rows = [above[r, at, :] * keep_above for r in range(height)]
        rows += [here[r, at, :] for r in range(height)]
        rows += [below[r, at, :] * keep_below for r in range(height)]
        for r in range(height):
            total = rows[r + REACH] * LAT_TAPS[REACH]
            for j in range(1, REACH + 1):
                total += (rows[r + REACH - j] + rows[r + REACH + j]) * LAT_TAPS[REACH + j]
            store(r, at, total)
        return carry

    lax.fori_loop(0, levels // 8, tile, 0, unroll=True)


def kernel(
    n_lat,
    n_lon,
    control_hbm,
    background_hbm,
    width_hbm,
    cells_hbm,
    owner_hbm,
    count_hbm,
    radiance_hbm,
    w1_hbm,
    b1_hbm,
    w2_hbm,
    b2_hbm,
    w3_hbm,
    b3_hbm,
    out_ref,
    width_ref,
    cells_ref,
    owner_ref,
    count_ref,
    b1_ref,
    b2_ref,
    b3_ref,
    control,
    background,
    radiance,
    w1,
    w2,
    w3,
    above,
    below,
    pack,
    from_left,
    from_right,
    flags,
    outgoing,
    observed,
    smooth,
    split_rows,
    split_back,
    rims,
    taps_high,
    taps_low,
    picks,
    band_high,
    band_low,
    back_rows,
    slot_rows,
    act_one,
    act_two,
    grad_two,
    grad_one,
    emitted,
    misfit,
    w2_turned,
    w3_turned,
    taps_turned,
    landed,
    landed_send,
    rim_send,
    above_back,
    below_back,
    left_back,
    right_back,
    local_sem,
    flag_send,
    flag_recv,
    rad_send,
    rad_recv,
    halo_send,
    halo_recv,
    back_send,
    back_recv,
):
    height, levels, width = control.shape
    slots = n_lat * BLOCK_COLS
    main = height * width
    side = height * REACH
    me = lax.axis_index("lat")
    col = lax.axis_index("lon")
    lat_at = {d: lax.rem(me + d + n_lat, n_lat) for d in (-1, 0, 1)}
    lon_at = {d: lax.rem(col + d + n_lon, n_lon) for d in (-1, 1)}

    n_row = 8 if n_lat % 16 == 0 else 2
    n_far = n_lat // n_row
    far = me // n_row
    near = me - far * n_row
    rings = by_distance(n_far)
    send_parts = min(SEND_PARTS, n_far)
    back_parts = min(BACK_PARTS, n_far)
    reaches = [(df, dn) for df in rings[::-1] for dn in range(n_row) if df or dn]
    reaches.sort(key=lambda d: -min(d[0], n_far - d[0]) - min(d[1], n_row - d[1]) / 2)

    def peer(df, dn):
        return lax.rem(far + df, n_far) * n_row + lax.rem(near + dn, n_row)

    barrier = pltpu.get_barrier_semaphore()
    for df, dn in reaches:
        pl.semaphore_signal(barrier, inc=1, device_id=(peer(df, dn), col), device_id_type=MESH)
    for dl in (-1, 0, 1):
        for dq in (-1, 1):
            pl.semaphore_signal(
                barrier, inc=1, device_id=(lat_at[dl], lon_at[dq]), device_id_type=MESH
            )

    loads = [
        pltpu.make_async_copy(source, target, local_sem.at[k])
        for k, (source, target) in enumerate(
            (
                (owner_hbm, owner_ref),
                (cells_hbm, cells_ref),
                (width_hbm, width_ref),
                (control_hbm, control),
                (background_hbm, background),
                (count_hbm, count_ref),
                (radiance_hbm, radiance),
                (w1_hbm, w1),
                (b1_hbm, b1_ref),
                (w2_hbm, w2),
                (b2_hbm, b2_ref),
                (w3_hbm, w3),
                (b3_hbm, b3_ref),
            )
        )
    ]
    for load in loads[:4]:
        load.start()

    n_slots = owner_ref.shape[1]
    for load in loads[:3]:
        load.wait()
    diag = iota((n_slots, n_slots), 0) == iota((n_slots, n_slots), 1)

    def upright(row):
        return jnp.sum(jnp.where(diag, row, 0), axis=1, keepdims=True)

    owner_col = upright(owner_ref[...])
    cells_col = upright(cells_ref[...])
    flags[pl.ds(me, 1)] = jnp.sum(
        (owner_col == iota((n_slots, 128), 1)).astype(F32), axis=0, keepdims=True
    ).reshape(1, 1, 128)

    loads[3].wait()
    lane = iota((levels, width), 1)
    per = width // REACH
    for k, start in enumerate((0, width - REACH)):
        for group in range(height // per):
            packed = jnp.zeros((levels, width), F32)
            for r in range(per):
                shift = (r * REACH - start) % width
                value = control[group * per + r]
                value = pltpu.roll(value, shift, 1) if shift else value
                packed = jnp.where(lane // REACH == r, value, packed)
            pack[k, group] = packed

    pl.semaphore_wait(barrier, n_lat - 1 + 6)

    def side_copies(left_src, right_src, left_dst, right_dst, send, recv):
        copies = []
        for dl in (-1, 0, 1):
            k = dl + 1
            copies.append(
                pltpu.make_async_remote_copy(
                    left_src, right_dst.at[1 - dl], send.at[k], recv.at[k],
                    (lat_at[dl], lon_at[-1]), MESH,
                )
            )
            copies.append(
                pltpu.make_async_remote_copy(
                    right_src, left_dst.at[1 - dl], send.at[k + 3], recv.at[k + 3],
                    (lat_at[dl], lon_at[1]), MESH,
                )
            )
        return copies

    def band_copies(source, above_dst, below_dst, send, recv, k):
        return [
            pltpu.make_async_remote_copy(
                source, below_dst, send.at[k], recv.at[k], (lat_at[-1], col), MESH
            ),
            pltpu.make_async_remote_copy(
                source, above_dst, send.at[k + 1], recv.at[k + 1], (lat_at[1], col), MESH
            ),
        ]

    flag_copies = [
        pltpu.make_async_remote_copy(
            flags.at[me], flags.at[me], flag_send.at[df * n_row + dn],
            flag_recv.at[df * n_row + dn], (peer(df, dn), col), MESH,
        )
        for df, dn in reaches
    ]

    def rad_copy(df, dn):
        source = rings[::-1].index(df) * n_row + lax.rem(near + dn, n_row)
        place = rings.index((n_far - df) % n_far) * n_row + near
        return pltpu.make_async_remote_copy(
            outgoing.at[source], observed.at[place], rad_send.at[df * n_row + dn],
            rad_recv.at[df * n_row + dn], (peer(df, dn), col), MESH,
        )

    for copy in flag_copies:
        copy.start()
    halo = band_copies(control, above, below, halo_send, halo_recv, 6)
    halo += side_copies(pack.at[0], pack.at[1], from_left, from_right, halo_send, halo_recv)
    for copy in halo:
        copy.start()
    for load in loads[4:]:
        load.start()

    lane_o = iota((1, slots), 1) // BLOCK_COLS
    owner_o = lax.rem(choose(lane_o // n_row, rings) + far, n_far) * n_row + lane_o % n_row
    mine = owner_col == owner_o
    cell = jnp.sum(jnp.where(mine, cells_col, 0), axis=0, keepdims=True)
    live = jnp.sum(mine.astype(F32), axis=0, keepdims=True)
    groups = width // BLOCK_COLS
    row_of = cell // groups
    lane_x = iota((1, slots), 1)
    place = (cell - row_of * groups) * BLOCK_COLS + lane_x % BLOCK_COLS
    spread = jnp.zeros((1, slots), F32)
    for r in range(height):
        spread += jnp.where(row_of == r, width_ref[r].astype(F32), 0.0)
    offset = iota((40, slots), 0).astype(F32) - REACH
    squares = jnp.sum(
        jnp.where(offset <= REACH, jnp.exp(-offset * offset / (spread * spread)), 0.0),
        axis=0,
        keepdims=True,
    )
    scale = live / jnp.sqrt(squares)
    rate = -0.5 / (spread * spread)

    def taps_at(column):
        away = (column - place).astype(F32)
        return jnp.where(jnp.abs(away) <= REACH, jnp.exp(away * away * rate) * scale, 0.0)

    column = iota((width, slots), 0)
    tap_high, tap_low = split_two(taps_at(column))
    pick = jnp.where(column == place, live, 0.0).astype(BF16)

    def lay(r, carry):
        rows = pl.ds(pl.multiple_of(r * width, width), width)
        keep = jnp.where(row_of == r, 1.0, 0.0).astype(BF16)
        taps_high[rows, :] = tap_high * keep
        taps_low[rows, :] = tap_low * keep
        picks[rows, :] = pick * keep
        return carry

    lax.fori_loop(0, height, lay, 0, unroll=True)
    rim = iota((side, slots), 0)
    for k, start in enumerate((-REACH, width)):
        value = jnp.where(rim // REACH == row_of, taps_at(rim % REACH + start), 0.0)
        high, low = split_two(value)
        taps_high[pl.ds(main + k * side, side), :] = high
        taps_low[pl.ds(main + k * side, side), :] = low

    rim_in = iota((3 * side, side), 0)
    rim_out = iota((3 * side, side), 1)
    away = (rim_in // REACH - height - rim_out // REACH).astype(F32)
    band = jnp.exp(away * away * (-0.5 / LAT_SIGMA**2)) * LAT_NORM
    band = jnp.where((jnp.abs(away) <= REACH) & (rim_in % REACH == rim_out % REACH), band, 0.0)
    high, low = split_two(band)
    band_high[...] = high
    band_low[...] = low

    loads[4].wait()
    for r in range(height):
        value = background[r]
        high, rest = split_two(value)
        middle = rest
        low = (value - high.astype(F32) - middle.astype(F32)).astype(BF16)
        lanes = pl.ds(r * width, width)
        split_back[pl.ds(0, levels), lanes] = high
        split_back[pl.ds(levels, levels), lanes] = middle
        split_back[pl.ds(2 * levels, levels), lanes] = low
    gathered = dot(split_back[...], picks[...])
    back_rows[...] = (
        gathered[:levels] + gathered[levels : 2 * levels] + gathered[2 * levels :]
    )

    for load in loads[5:7]:
        load.wait()
    n_recv = radiance.shape[0] // BLOCK_COLS
    channels = radiance.shape[1]
    counts = jnp.sum(
        jnp.where(
            iota((n_recv * BLOCK_COLS, n_recv), 1)
            == iota((n_recv * BLOCK_COLS, n_recv), 0) // BLOCK_COLS,
            count_ref[...],
            0,
        ),
        axis=1,
        keepdims=True,
    )
    seen = jnp.where(
        iota((n_recv * BLOCK_COLS, channels), 1) < counts, radiance[...].astype(F32), UNSEEN
    ).astype(BF16)

    for copy in flag_copies:
        copy.wait_recv()
    table = flags[...].reshape(n_lat, 128)
    sent = jnp.sum(
        jnp.where(iota((n_lat, 128), 1) == me, table, 0.0), axis=1, keepdims=True
    )
    sent = jnp.broadcast_to(sent, (n_lat, n_recv * BLOCK_COLS)).astype(BF16)
    piece = slots // send_parts
    rads = {}
    for part in range(send_parts):
        row_o = (iota((piece, n_lat), 0) + part * piece) // BLOCK_COLS
        source = lax.rem(choose(row_o // n_row, rings[::-1]) + far, n_far) * n_row + row_o % n_row
        entry = iota((piece, n_lat), 1)
        present = dot((entry == source).astype(BF16), sent)
        arrival = dot((entry < source).astype(BF16), sent)
        slot_x = iota((piece, n_recv * BLOCK_COLS), 1)
        row_x = iota((piece, n_recv * BLOCK_COLS), 0)
        select = (
            (present > 0.5)
            & (arrival == (slot_x // BLOCK_COLS).astype(F32))
            & (slot_x % BLOCK_COLS == row_x % BLOCK_COLS)
        )
        outgoing[pl.ds(part * (n_lat // send_parts), n_lat // send_parts)] = (
            dot(select.astype(BF16), seen).reshape(n_lat // send_parts, BLOCK_COLS, channels).astype(BF16)
        )
        for df, dn in reaches:
            if rings[::-1].index(df) * send_parts // n_far == part:
                rads[df, dn] = rad_copy(df, dn)
                rads[df, dn].start()
    own = pltpu.make_async_copy(
        outgoing.at[(n_far - 1) * n_row + near], observed.at[near], local_sem.at[len(loads)]
    )
    own.start()

    keep_above = jnp.where(me > 0, 1.0, 0.0).astype(F32)
    keep_below = jnp.where(me < n_lat - 1, 1.0, 0.0).astype(F32)
    for copy in halo:
        copy.wait_recv()

    def keep_smooth(r, at, value):
        smooth[r, at, :] = value

    smooth_rows(above, control, below, keep_above, keep_below, height, levels, keep_smooth)
    for r in range(height):
        high, low = split_two(smooth[r])
        split_rows[pl.ds(0, levels), pl.ds(r * width, width)] = high
        split_rows[pl.ds(levels, levels), pl.ds(r * width, width)] = low
    keeps = (keep_above, 1.0, keep_below)
    for k, ref in enumerate((from_left, from_right)):
        for b in range(3):
            for g in range(side // width):
                high, low = split_two(ref[b, g] * keeps[b])
                lanes = pl.ds(b * side + g * width, width)
                rims[pl.ds(k * levels, levels), lanes] = high
                rims[pl.ds((2 + k) * levels, levels), lanes] = low
    crossed = dot(rims[...], band_high[...])
    crossed = (
        crossed[: 2 * levels]
        + crossed[2 * levels :]
        + dot(rims[pl.ds(0, 2 * levels), :], band_low[...])
    )
    for k in range(2):
        high, low = split_two(crossed[k * levels : (k + 1) * levels])
        lanes = pl.ds(main + k * side, side)
        split_rows[pl.ds(0, levels), lanes] = high
        split_rows[pl.ds(levels, levels), lanes] = low
    total = dot(split_rows[...], taps_high[...])
    profile = (
        total[:levels]
        + total[levels:]
        + dot(split_rows[pl.ds(0, levels), :], taps_low[...])
        + back_rows[...]
    )
    slot_rows[...] = profile.T.astype(BF16)

    for load in loads[7:]:
        load.wait()
    tile = 256
    hidden = w2.shape[0]

    def lanes_of(n):
        return pl.ds(pl.multiple_of(n * tile, tile), tile)

    def first(n, carry):
        at = lanes_of(n)
        act_one[:, at] = jnp.tanh(dot(slot_rows[...], w1[:, at]) + b1_ref[:, at]).astype(BF16)
        return carry

    def second(n, carry):
        at = lanes_of(n)
        act_two[:, at] = jnp.tanh(dot(act_one[...], w2[:, at]) + b2_ref[:, at]).astype(BF16)
        return carry

    lax.fori_loop(0, hidden // tile, first, 0, unroll=True)
    lax.fori_loop(0, hidden // tile, second, 0, unroll=True)
    emitted[...] = dot(act_two[...], w3[...]) + b3_ref[...]

    w2_turned[...] = w2[...].T
    w3_turned[...] = w3[...].T
    taps_turned[...] = taps_high[...].T

    own.wait()
    piece = slots // back_parts
    for part in range(back_parts):
        for df, dn in reaches:
            if rings.index((n_far - df) % n_far) * back_parts // n_far == part:
                rads[df, dn].wait_recv()
        rows = pl.ds(part * piece, piece)
        target = observed[pl.ds(part * (n_lat // back_parts), n_lat // back_parts)].astype(F32).reshape(piece, channels)
        misfit[...] = jnp.where(
            target < 0.5 * UNSEEN, emitted[rows, :] - target, 0.0
        ).astype(BF16)

        def second_back(n, carry):
            at = lanes_of(n)
            value = act_two[rows, at].astype(F32)
            grad_two[:, at] = (dot(misfit[...], w3_turned[:, at]) * (1.0 - value * value)).astype(BF16)
            return carry

        def first_back(n, carry):
            at = lanes_of(n)
            value = act_one[rows, at].astype(F32)
            grad_one[rows, at] = (
                dot(grad_two[...], w2_turned[:, at]) * (1.0 - value * value)
            ).astype(BF16)
            return carry

        lax.fori_loop(0, hidden // tile, second_back, 0, unroll=True)
        lax.fori_loop(0, hidden // tile, first_back, 0, unroll=True)
    sensitivity = dot(w1[...], grad_one[...], NT).astype(BF16)

    edges = dot(sensitivity, taps_turned[:, pl.ds(main, 2 * side)]).astype(BF16)
    for k in range(2):
        rim_send[k] = edges[:, k * side : (k + 1) * side]
    sides = side_copies(
        rim_send.at[0], rim_send.at[1], left_back, right_back, back_send, back_recv
    )
    for copy in sides:
        copy.start()
    bands = []
    chunk = height // CHUNKS
    for part in range(CHUNKS):
        rows = pl.ds(part * chunk, chunk)
        spreadout = dot(sensitivity, taps_turned[:, pl.ds(part * chunk * width, chunk * width)])
        for r in range(chunk):
            value = spreadout[:, r * width : (r + 1) * width]
            landed[part * chunk + r] = value
            landed_send[part * chunk + r] = value.astype(BF16)
        bands += band_copies(
            landed_send.at[rows], above_back.at[rows], below_back.at[rows],
            back_send, back_recv, 6 + 2 * part,
        )
        for copy in bands[-2:]:
            copy.start()

    def own_rows(t, carry):
        at = pl.ds(pl.multiple_of(t * 8, 8), 8)
        values = [landed[r, at, :] for r in range(height)]
        for r in range(height):
            total = values[r] * LAT_TAPS[REACH]
            for j in range(1, height):
                pair = [values[k] for k in (r - j, r + j) if 0 <= k < height]
                if pair:
                    total += sum(pair[1:], pair[0]) * LAT_TAPS[REACH + j]
            smooth[r, at, :] = total
        return carry

    lax.fori_loop(0, levels // 8, own_rows, 0, unroll=True)
    for copy in flag_copies + list(rads.values()) + halo:
        copy.wait_send()
    for copy in bands:
        copy.wait_recv()
    for r in range(height):
        above[r] = above_back[r].astype(F32) * keep_above
        below[r] = below_back[r].astype(F32) * keep_below

    def other_rows(t, carry):
        at = pl.ds(pl.multiple_of(t * 8, 8), 8)
        upper = [above[r, at, :] for r in range(height)]
        lower = [below[r, at, :] for r in range(height)]
        for r in range(height):
            total = smooth[r, at, :]
            for k in range(height):
                if r + height - k <= REACH:
                    total += upper[k] * LAT_TAPS[REACH + r + height - k]
                if k + height - r <= REACH:
                    total += lower[k] * LAT_TAPS[REACH + k + height - r]
            smooth[r, at, :] = total
        return carry

    lax.fori_loop(0, levels // 8, other_rows, 0, unroll=True)
    for copy in sides:
        copy.wait_recv()
    for k, ref in enumerate((left_back, right_back)):
        for b in range(3):
            rims[pl.ds(k * levels, levels), pl.ds(b * side, side)] = (
                ref[b].astype(F32) * keeps[b]
            ).astype(BF16)
    crossed = dot(rims[pl.ds(0, 2 * levels), :], band_high[...])
    for r in range(height):
        at = slice(r // per * width, (r // per + 1) * width)
        low_cols = crossed[:levels, at]
        high_cols = crossed[levels:, at]
        shift = (-(r % per) * REACH) % width
        low_cols = pltpu.roll(low_cols, shift, 1) if shift else low_cols
        shift = (width - REACH - (r % per) * REACH) % width
        high_cols = pltpu.roll(high_cols, shift, 1) if shift else high_cols
        edge = jnp.where(lane < REACH, low_cols, jnp.where(lane >= width - REACH, high_cols, 0.0))
        out_ref[r] = smooth[r] + edge

    for copy in sides + bands:
        copy.wait_send()


def shards(
    n_lat,
    n_lon,
    control,
    background,
    lon_width,
    block_cells,
    block_owner,
    channel_count,
    radiance,
    in_weight,
    in_bias,
    mid_weight,
    mid_bias,
    out_weight,
    out_bias,
):
    height, levels, width = control.shape
    hidden = mid_weight.shape[0]
    channels, recv_cols = radiance.shape
    slots = n_lat * BLOCK_COLS
    n_far = n_lat // (8 if n_lat % 16 == 0 else 2)
    main = height * width
    side = height * REACH
    per_side = side // width
    dma = pltpu.SemaphoreType.DMA
    vmem = pltpu.VMEM
    hbm_spec = pl.BlockSpec(memory_space=pltpu.HBM)
    vmem_spec = pl.BlockSpec(memory_space=pltpu.VMEM)
    grid = (height, levels, width)
    adjoint = pl.pallas_call(
        functools.partial(kernel, n_lat, n_lon),
        out_shape=jax.ShapeDtypeStruct(grid, F32),
        in_specs=[hbm_spec] * 13,
        out_specs=vmem_spec,
        scratch_shapes=[
            pltpu.SMEM(lon_width.shape, I32),
            vmem((1, block_cells.shape[0]), I32),
            vmem((1, block_owner.shape[0]), I32),
            vmem((1, channel_count.shape[0]), I32),
            vmem((1, hidden), F32),
            vmem((1, hidden), F32),
            vmem((1, channels), F32),
            vmem(grid, F32),
            vmem(grid, F32),
            vmem((recv_cols, channels), BF16),
            vmem((levels, hidden), BF16),
            vmem((hidden, hidden), BF16),
            vmem((hidden, channels), BF16),
            vmem(grid, F32),
            vmem(grid, F32),
            vmem((2, per_side, levels, width), F32),
            vmem((3, per_side, levels, width), F32),
            vmem((3, per_side, levels, width), F32),
            vmem((n_lat, 1, 128), F32),
            vmem((n_lat, BLOCK_COLS, channels), BF16),
            vmem((n_lat, BLOCK_COLS, channels), BF16),
            vmem(grid, F32),
            vmem((2 * levels, main + 2 * side), BF16),
            vmem((3 * levels, main), BF16),
            vmem((4 * levels, 3 * side), BF16),
            vmem((main + 2 * side, slots), BF16),
            vmem((main + 2 * side, slots), BF16),
            vmem((main, slots), BF16),
            vmem((3 * side, side), BF16),
            vmem((3 * side, side), BF16),
            vmem((levels, slots), F32),
            vmem((slots, levels), BF16),
            vmem((slots, hidden), BF16),
            vmem((slots, hidden), BF16),
            vmem((slots // min(BACK_PARTS, n_far), hidden), BF16),
            vmem((slots, hidden), BF16),
            vmem((slots, channels), F32),
            vmem((slots // min(BACK_PARTS, n_far), channels), BF16),
            vmem((hidden, hidden), BF16),
            vmem((channels, hidden), BF16),
            vmem((slots, main + 2 * side), BF16),
            vmem(grid, F32),
            vmem(grid, BF16),
            vmem((2, levels, side), BF16),
            vmem(grid, BF16),
            vmem(grid, BF16),
            vmem((3, levels, side), BF16),
            vmem((3, levels, side), BF16),
            dma((14,)),
            dma((n_lat,)),
            dma((n_lat,)),
            dma((n_lat,)),
            dma((n_lat,)),
            dma((8,)),
            dma((8,)),
            dma((6 + 2 * CHUNKS,)),
            dma((6 + 2 * CHUNKS,)),
        ],
        compiler_params=pltpu.CompilerParams(
            collective_id=0, has_side_effects=True, vmem_limit_bytes=36 * 1024 * 1024
        ),
    )(
        *(
            pltpu.with_memory_space_constraint(value, pltpu.HBM)
            for value in (
                control,
                background,
                lon_width,
                block_cells.T,
                block_owner.T,
                channel_count.T,
                radiance.T,
                in_weight,
                in_bias.reshape(1, -1),
                mid_weight,
                mid_bias.reshape(1, -1),
                out_weight,
                out_bias.reshape(1, -1),
            )
        )
    )
    return control + adjoint


def solution(mesh):
    return jax.shard_map(
        functools.partial(shards, mesh.shape["lat"], mesh.shape["lon"]),
        mesh=mesh,
        in_specs=(
            P("lat", None, "lon"),
            P("lat", None, "lon"),
            P("lat"),
            P("lat", "lon"),
            P("lat", "lon"),
            P("lat", "lon"),
            P("lat", "lon"),
            P(),
            P(),
            P(),
            P(),
            P(),
            P(),
        ),
        out_specs=P("lat", None, "lon"),
        check_vma=False,
    )
```

```python
import functools

import jax
import jax.numpy as jnp
import numpy as np
from jax import lax
from jax.experimental import pallas as pl
from jax.experimental.pallas import tpu as pltpu
from jax.sharding import PartitionSpec as P

REACH = 16
BLOCK_COLS = 8
LAT_SIGMA = 8.0
CHUNKS = 4
SEND_PARTS = 2
BACK_PARTS = 1
UNSEEN = 32768.0
MESH = pl.DeviceIdType.MESH
F32 = jnp.float32
BF16 = jnp.bfloat16
I32 = jnp.int32
NN = (((1,), (0,)), ((), ()))
NT = (((1,), (1,)), ((), ()))

steps = np.arange(-REACH, REACH + 1).astype(np.float64)
raw = np.exp(-steps * steps / (2.0 * LAT_SIGMA**2))
LAT_TAPS = [float(v) for v in raw / np.sqrt(np.sum(raw * raw))]
LAT_NORM = float(1.0 / np.sqrt(np.sum(raw * raw)))


def dot(a, b, dims=NN):
    return lax.dot_general(a, b, dims, preferred_element_type=F32)


def split_two(value):
    high = value.astype(BF16)
    return high, (value - high.astype(F32)).astype(BF16)


def iota(shape, dim):
    return lax.broadcasted_iota(I32, shape, dim)


def by_distance(count):
    return sorted(range(count), key=lambda d: (min(d, count - d), d))


def choose(index, values):
    chosen = jnp.zeros_like(index)
    for k, value in enumerate(values):
        chosen = jnp.where(index == k, value, chosen)
    return chosen


def smooth_rows(above, here, below, keep_above, keep_below, height, levels, store):
    def tile(t, carry):
        at = pl.ds(pl.multiple_of(t * 8, 8), 8)
        rows = [above[r, at, :] * keep_above for r in range(height)]
        rows += [here[r, at, :] for r in range(height)]
        rows += [below[r, at, :] * keep_below for r in range(height)]
        for r in range(height):
            total = rows[r + REACH] * LAT_TAPS[REACH]
            for j in range(1, REACH + 1):
                total += (rows[r + REACH - j] + rows[r + REACH + j]) * LAT_TAPS[REACH + j]
            store(r, at, total)
        return carry

    lax.fori_loop(0, levels // 8, tile, 0, unroll=True)


def kernel(
    n_lat,
    n_lon,
    control_hbm,
    background_hbm,
    width_hbm,
    cells_hbm,
    owner_hbm,
    count_hbm,
    radiance_hbm,
    w1_hbm,
    b1_hbm,
    w2_hbm,
    b2_hbm,
    w3_hbm,
    b3_hbm,
    out_ref,
    width_ref,
    cells_ref,
    owner_ref,
    count_ref,
    b1_ref,
    b2_ref,
    b3_ref,
    control,
    background,
    radiance,
    w1,
    w2,
    w3,
    above,
    below,
    pack,
    from_left,
    from_right,
    flags,
    outgoing,
    observed,
    smooth,
    split_rows,
    split_back,
    rims,
    taps_high,
    taps_low,
    picks,
    band_high,
    band_low,
    back_rows,
    slot_rows,
    act_one,
    act_two,
    grad_two,
    grad_one,
    emitted,
    misfit,
    w1_turned,
    w2_turned,
    w3_turned,
    taps_turned,
    landed,
    landed_send,
    rim_send,
    above_back,
    below_back,
    left_back,
    right_back,
    local_sem,
    flag_send,
    flag_recv,
    rad_send,
    rad_recv,
    halo_send,
    halo_recv,
    back_send,
    back_recv,
):
    height, levels, width = control.shape
    slots = n_lat * BLOCK_COLS
    main = height * width
    side = height * REACH
    me = lax.axis_index("lat")
    col = lax.axis_index("lon")
    lat_at = {d: lax.rem(me + d + n_lat, n_lat) for d in (-1, 0, 1)}
    lon_at = {d: lax.rem(col + d + n_lon, n_lon) for d in (-1, 1)}

    n_row = 8 if n_lat % 16 == 0 else 2
    n_far = n_lat // n_row
    far = me // n_row
    near = me - far * n_row
    rings = by_distance(n_far)
    send_parts = min(SEND_PARTS, n_far)
    back_parts = min(BACK_PARTS, n_far)
    reaches = [(df, dn) for df in rings[::-1] for dn in range(n_row) if df or dn]
    reaches.sort(key=lambda d: -min(d[0], n_far - d[0]) - min(d[1], n_row - d[1]) / 2)

    def peer(df, dn):
        return lax.rem(far + df, n_far) * n_row + lax.rem(near + dn, n_row)

    barrier = pltpu.get_barrier_semaphore()
    for df, dn in reaches:
        pl.semaphore_signal(barrier, inc=1, device_id=(peer(df, dn), col), device_id_type=MESH)
    for dl in (-1, 0, 1):
        for dq in (-1, 1):
            pl.semaphore_signal(
                barrier, inc=1, device_id=(lat_at[dl], lon_at[dq]), device_id_type=MESH
            )

    loads = [
        pltpu.make_async_copy(source, target, local_sem.at[k])
        for k, (source, target) in enumerate(
            (
                (owner_hbm, owner_ref),
                (cells_hbm, cells_ref),
                (width_hbm, width_ref),
                (control_hbm, control),
                (background_hbm, background),
                (count_hbm, count_ref),
                (radiance_hbm, radiance),
                (w1_hbm, w1),
                (b1_hbm, b1_ref),
                (w2_hbm, w2),
                (b2_hbm, b2_ref),
                (w3_hbm, w3),
                (b3_hbm, b3_ref),
            )
        )
    ]
    for load in loads[:4]:
        load.start()

    n_slots = owner_ref.shape[1]
    for load in loads[:3]:
        load.wait()
    diag = iota((n_slots, n_slots), 0) == iota((n_slots, n_slots), 1)

    def upright(row):
        return jnp.sum(jnp.where(diag, row, 0), axis=1, keepdims=True)

    owner_col = upright(owner_ref[...])
    cells_col = upright(cells_ref[...])
    flags[pl.ds(me, 1)] = jnp.sum(
        (owner_col == iota((n_slots, 128), 1)).astype(F32), axis=0, keepdims=True
    ).reshape(1, 1, 128)

    pl.semaphore_wait(barrier, n_lat - 1 + 6)

    def side_copies(left_src, right_src, left_dst, right_dst, send, recv):
        copies = []
        for dl in (-1, 1, 0):
            k = dl + 1
            copies.append(
                pltpu.make_async_remote_copy(
                    left_src, right_dst.at[1 - dl], send.at[k], recv.at[k],
                    (lat_at[dl], lon_at[-1]), MESH,
                )
            )
            copies.append(
                pltpu.make_async_remote_copy(
                    right_src, left_dst.at[1 - dl], send.at[k + 3], recv.at[k + 3],
                    (lat_at[dl], lon_at[1]), MESH,
                )
            )
        return copies

    def band_copies(source, above_dst, below_dst, send, recv, k):
        return [
            pltpu.make_async_remote_copy(
                source, below_dst, send.at[k], recv.at[k], (lat_at[-1], col), MESH
            ),
            pltpu.make_async_remote_copy(
                source, above_dst, send.at[k + 1], recv.at[k + 1], (lat_at[1], col), MESH
            ),
        ]

    flag_copies = [
        pltpu.make_async_remote_copy(
            flags.at[me], flags.at[me], flag_send.at[df * n_row + dn],
            flag_recv.at[df * n_row + dn], (peer(df, dn), col), MESH,
        )
        for df, dn in reaches
    ]

    def rad_copy(df, dn):
        source = rings[::-1].index(df) * n_row + lax.rem(near + dn, n_row)
        place = rings.index((n_far - df) % n_far) * n_row + near
        return pltpu.make_async_remote_copy(
            outgoing.at[source], observed.at[place], rad_send.at[df * n_row + dn],
            rad_recv.at[df * n_row + dn], (peer(df, dn), col), MESH,
        )

    for copy in flag_copies:
        copy.start()
    loads[3].wait()
    lane = iota((levels, width), 1)
    per = width // REACH
    for k, start in enumerate((0, width - REACH)):
        for group in range(height // per):
            packed = jnp.zeros((levels, width), F32)
            for r in range(per):
                shift = (r * REACH - start) % width
                value = control[group * per + r]
                value = pltpu.roll(value, shift, 1) if shift else value
                packed = jnp.where(lane // REACH == r, value, packed)
            pack[k, group] = packed

    halo = band_copies(control, above, below, halo_send, halo_recv, 6)
    halo += side_copies(pack.at[0], pack.at[1], from_left, from_right, halo_send, halo_recv)
    for copy in halo:
        copy.start()
    for load in loads[4:]:
        load.start()

    lane_o = iota((1, slots), 1) // BLOCK_COLS
    owner_o = lax.rem(choose(lane_o // n_row, rings) + far, n_far) * n_row + lane_o % n_row
    mine = owner_col == owner_o
    cell = jnp.sum(jnp.where(mine, cells_col, 0), axis=0, keepdims=True)
    live = jnp.sum(mine.astype(F32), axis=0, keepdims=True)
    groups = width // BLOCK_COLS
    row_of = cell // groups
    lane_x = iota((1, slots), 1)
    place = (cell - row_of * groups) * BLOCK_COLS + lane_x % BLOCK_COLS
    spread = jnp.zeros((1, slots), F32)
    for r in range(height):
        spread += jnp.where(row_of == r, width_ref[r].astype(F32), 0.0)
    offset = iota((40, slots), 0).astype(F32) - REACH
    squares = jnp.sum(
        jnp.where(offset <= REACH, jnp.exp(-offset * offset / (spread * spread)), 0.0),
        axis=0,
        keepdims=True,
    )
    scale = live / jnp.sqrt(squares)
    rate = -0.5 / (spread * spread)

    def taps_at(column):
        away = (column - place).astype(F32)
        return jnp.where(jnp.abs(away) <= REACH, jnp.exp(away * away * rate) * scale, 0.0)

    column = iota((width, slots), 0)
    tap_high, tap_low = split_two(taps_at(column))
    pick = jnp.where(column == place, live, 0.0).astype(BF16)

    def lay(r, carry):
        rows = pl.ds(pl.multiple_of(r * width, width), width)
        keep = jnp.where(row_of == r, 1.0, 0.0).astype(BF16)
        taps_high[rows, :] = tap_high * keep
        taps_low[rows, :] = tap_low * keep
        picks[rows, :] = pick * keep
        return carry

    lax.fori_loop(0, height, lay, 0, unroll=True)
    rim = iota((side, slots), 0)
    for k, start in enumerate((-REACH, width)):
        value = jnp.where(rim // REACH == row_of, taps_at(rim % REACH + start), 0.0)
        high, low = split_two(value)
        taps_high[pl.ds(main + k * side, side), :] = high
        taps_low[pl.ds(main + k * side, side), :] = low

    rim_in = iota((3 * side, side), 0)
    rim_out = iota((3 * side, side), 1)
    away = (rim_in // REACH - height - rim_out // REACH).astype(F32)
    band = jnp.exp(away * away * (-0.5 / LAT_SIGMA**2)) * LAT_NORM
    band = jnp.where((jnp.abs(away) <= REACH) & (rim_in % REACH == rim_out % REACH), band, 0.0)
    high, low = split_two(band)
    band_high[...] = high
    band_low[...] = low

    loads[4].wait()
    for r in range(height):
        value = background[r]
        high, rest = split_two(value)
        middle = rest
        low = (value - high.astype(F32) - middle.astype(F32)).astype(BF16)
        lanes = pl.ds(r * width, width)
        split_back[pl.ds(0, levels), lanes] = high
        split_back[pl.ds(levels, levels), lanes] = middle
        split_back[pl.ds(2 * levels, levels), lanes] = low
    gathered = dot(split_back[...], picks[...])
    back_rows[...] = (
        gathered[:levels] + gathered[levels : 2 * levels] + gathered[2 * levels :]
    )

    for load in loads[5:7]:
        load.wait()
    n_recv = radiance.shape[0] // BLOCK_COLS
    channels = radiance.shape[1]
    counts = jnp.sum(
        jnp.where(
            iota((n_recv * BLOCK_COLS, n_recv), 1)
            == iota((n_recv * BLOCK_COLS, n_recv), 0) // BLOCK_COLS,
            count_ref[...],
            0,
        ),
        axis=1,
        keepdims=True,
    )
    seen = jnp.where(
        iota((n_recv * BLOCK_COLS, channels), 1) < counts, radiance[...].astype(F32), UNSEEN
    ).astype(BF16)

    for copy in flag_copies:
        copy.wait_recv()
    table = flags[...].reshape(n_lat, 128)
    sent = jnp.sum(
        jnp.where(iota((n_lat, 128), 1) == me, table, 0.0), axis=1, keepdims=True
    )
    sent = jnp.broadcast_to(sent, (n_lat, n_recv * BLOCK_COLS)).astype(BF16)
    piece = slots // send_parts
    rads = {}
    for part in range(send_parts):
        row_o = (iota((piece, n_lat), 0) + part * piece) // BLOCK_COLS
        source = lax.rem(choose(row_o // n_row, rings[::-1]) + far, n_far) * n_row + row_o % n_row
        entry = iota((piece, n_lat), 1)
        present = dot((entry == source).astype(BF16), sent)
        arrival = dot((entry < source).astype(BF16), sent)
        slot_x = iota((piece, n_recv * BLOCK_COLS), 1)
        row_x = iota((piece, n_recv * BLOCK_COLS), 0)
        select = (
            (present > 0.5)
            & (arrival == (slot_x // BLOCK_COLS).astype(F32))
            & (slot_x % BLOCK_COLS == row_x % BLOCK_COLS)
        )
        outgoing[pl.ds(part * (n_lat // send_parts), n_lat // send_parts)] = (
            dot(select.astype(BF16), seen).reshape(n_lat // send_parts, BLOCK_COLS, channels).astype(BF16)
        )
        for df, dn in reaches:
            if rings[::-1].index(df) * send_parts // n_far == part:
                rads[df, dn] = rad_copy(df, dn)
                rads[df, dn].start()
    own = pltpu.make_async_copy(
        outgoing.at[(n_far - 1) * n_row + near], observed.at[near], local_sem.at[len(loads)]
    )
    own.start()

    keep_above = jnp.where(me > 0, 1.0, 0.0).astype(F32)
    keep_below = jnp.where(me < n_lat - 1, 1.0, 0.0).astype(F32)
    for copy in halo:
        copy.wait_recv()

    def keep_smooth(r, at, value):
        smooth[r, at, :] = value

    smooth_rows(above, control, below, keep_above, keep_below, height, levels, keep_smooth)
    for r in range(height):
        high, low = split_two(smooth[r])
        split_rows[pl.ds(0, levels), pl.ds(r * width, width)] = high
        split_rows[pl.ds(levels, levels), pl.ds(r * width, width)] = low
    keeps = (keep_above, 1.0, keep_below)
    for k, ref in enumerate((from_left, from_right)):
        for b in range(3):
            for g in range(side // width):
                high, low = split_two(ref[b, g] * keeps[b])
                lanes = pl.ds(b * side + g * width, width)
                rims[pl.ds(k * levels, levels), lanes] = high
                rims[pl.ds((2 + k) * levels, levels), lanes] = low
    crossed = dot(rims[...], band_high[...])
    crossed = (
        crossed[: 2 * levels]
        + crossed[2 * levels :]
        + dot(rims[pl.ds(0, 2 * levels), :], band_low[...])
    )
    for k in range(2):
        high, low = split_two(crossed[k * levels : (k + 1) * levels])
        lanes = pl.ds(main + k * side, side)
        split_rows[pl.ds(0, levels), lanes] = high
        split_rows[pl.ds(levels, levels), lanes] = low
    total = dot(split_rows[...], taps_high[...])
    profile = (
        total[:levels]
        + total[levels:]
        + dot(split_rows[pl.ds(0, levels), :], taps_low[...])
        + back_rows[...]
    )
    slot_rows[...] = profile.T.astype(BF16)

    for load in loads[7:]:
        load.wait()
    tile = 256
    hidden = w2.shape[0]

    def lanes_of(n):
        return pl.ds(pl.multiple_of(n * tile, tile), tile)

    def first(n, carry):
        at = lanes_of(n)
        act_one[:, at] = jnp.tanh(dot(slot_rows[...], w1[:, at]) + b1_ref[:, at]).astype(BF16)
        return carry

    def second(n, carry):
        at = lanes_of(n)
        act_two[:, at] = jnp.tanh(dot(act_one[...], w2[:, at]) + b2_ref[:, at]).astype(BF16)
        return carry

    lax.fori_loop(0, hidden // tile, first, 0, unroll=True)
    lax.fori_loop(0, hidden // tile, second, 0, unroll=True)
    emitted[...] = dot(act_two[...], w3[...]) + b3_ref[...]

    w1_turned[...] = w1[...].T
    w2_turned[...] = w2[...].T
    w3_turned[...] = w3[...].T
    taps_turned[...] = taps_high[...].T

    own.wait()
    piece = slots // back_parts
    for part in range(back_parts):
        for df, dn in reaches:
            if rings.index((n_far - df) % n_far) * back_parts // n_far == part:
                rads[df, dn].wait_recv()
        rows = pl.ds(part * piece, piece)
        target = observed[pl.ds(part * (n_lat // back_parts), n_lat // back_parts)].astype(F32).reshape(piece, channels)
        misfit[...] = jnp.where(
            target < 0.5 * UNSEEN, emitted[rows, :] - target, 0.0
        ).astype(BF16)

        def second_back(n, carry):
            at = lanes_of(n)
            value = act_two[rows, at].astype(F32)
            grad_two[:, at] = (dot(misfit[...], w3_turned[:, at]) * (1.0 - value * value)).astype(BF16)
            return carry

        def first_back(n, carry):
            at = lanes_of(n)
            value = act_one[rows, at].astype(F32)
            grad_one[rows, at] = (
                dot(grad_two[...], w2_turned[:, at]) * (1.0 - value * value)
            ).astype(BF16)
            return carry

        lax.fori_loop(0, hidden // tile, second_back, 0, unroll=True)
        lax.fori_loop(0, hidden // tile, first_back, 0, unroll=True)
    sensitivity = dot(grad_one[...], w1_turned[...]).T.astype(BF16)

    edges = dot(sensitivity, taps_turned[:, pl.ds(main, 2 * side)]).astype(BF16)
    for k in range(2):
        rim_send[k] = edges[:, k * side : (k + 1) * side]
    sides = side_copies(
        rim_send.at[0], rim_send.at[1], left_back, right_back, back_send, back_recv
    )
    for copy in sides:
        copy.start()
    bands = []
    chunk = height // CHUNKS
    for part in range(CHUNKS):
        rows = pl.ds(part * chunk, chunk)
        spreadout = dot(sensitivity, taps_turned[:, pl.ds(part * chunk * width, chunk * width)])
        for r in range(chunk):
            value = spreadout[:, r * width : (r + 1) * width]
            landed[part * chunk + r] = value
            landed_send[part * chunk + r] = value.astype(BF16)
        bands += band_copies(
            landed_send.at[rows], above_back.at[rows], below_back.at[rows],
            back_send, back_recv, 6 + 2 * part,
        )
        for copy in bands[-2:]:
            copy.start()

    def own_rows(t, carry):
        at = pl.ds(pl.multiple_of(t * 8, 8), 8)
        values = [landed[r, at, :] for r in range(height)]
        for r in range(height):
            total = values[r] * LAT_TAPS[REACH]
            for j in range(1, height):
                pair = [values[k] for k in (r - j, r + j) if 0 <= k < height]
                if pair:
                    total += sum(pair[1:], pair[0]) * LAT_TAPS[REACH + j]
            smooth[r, at, :] = total
        return carry

    lax.fori_loop(0, levels // 8, own_rows, 0, unroll=True)
    for copy in flag_copies + list(rads.values()) + halo:
        copy.wait_send()
    for copy in bands:
        copy.wait_recv()
    for r in range(height):
        above[r] = above_back[r].astype(F32) * keep_above
        below[r] = below_back[r].astype(F32) * keep_below

    def other_rows(t, carry):
        at = pl.ds(pl.multiple_of(t * 8, 8), 8)
        upper = [above[r, at, :] for r in range(height)]
        lower = [below[r, at, :] for r in range(height)]
        for r in range(height):
            total = smooth[r, at, :]
            for k in range(height):
                if r + height - k <= REACH:
                    total += upper[k] * LAT_TAPS[REACH + r + height - k]
                if k + height - r <= REACH:
                    total += lower[k] * LAT_TAPS[REACH + k + height - r]
            smooth[r, at, :] = total
        return carry

    lax.fori_loop(0, levels // 8, other_rows, 0, unroll=True)
    for copy in sides:
        copy.wait_recv()
    for k, ref in enumerate((left_back, right_back)):
        for b in range(3):
            rims[pl.ds(k * levels, levels), pl.ds(b * side, side)] = (
                ref[b].astype(F32) * keeps[b]
            ).astype(BF16)
    crossed = dot(rims[pl.ds(0, 2 * levels), :], band_high[...])
    for r in range(height):
        at = slice(r // per * width, (r // per + 1) * width)
        low_cols = crossed[:levels, at]
        high_cols = crossed[levels:, at]
        shift = (-(r % per) * REACH) % width
        low_cols = pltpu.roll(low_cols, shift, 1) if shift else low_cols
        shift = (width - REACH - (r % per) * REACH) % width
        high_cols = pltpu.roll(high_cols, shift, 1) if shift else high_cols
        edge = jnp.where(lane < REACH, low_cols, jnp.where(lane >= width - REACH, high_cols, 0.0))
        out_ref[r] = smooth[r] + edge

    for copy in sides + bands:
        copy.wait_send()


def shards(
    n_lat,
    n_lon,
    control,
    background,
    lon_width,
    block_cells,
    block_owner,
    channel_count,
    radiance,
    in_weight,
    in_bias,
    mid_weight,
    mid_bias,
    out_weight,
    out_bias,
):
    height, levels, width = control.shape
    hidden = mid_weight.shape[0]
    channels, recv_cols = radiance.shape
    slots = n_lat * BLOCK_COLS
    n_far = n_lat // (8 if n_lat % 16 == 0 else 2)
    main = height * width
    side = height * REACH
    per_side = side // width
    dma = pltpu.SemaphoreType.DMA
    vmem = pltpu.VMEM
    hbm_spec = pl.BlockSpec(memory_space=pltpu.HBM)
    vmem_spec = pl.BlockSpec(memory_space=pltpu.VMEM)
    grid = (height, levels, width)
    adjoint = pl.pallas_call(
        functools.partial(kernel, n_lat, n_lon),
        out_shape=jax.ShapeDtypeStruct(grid, F32),
        in_specs=[hbm_spec] * 13,
        out_specs=vmem_spec,
        scratch_shapes=[
            pltpu.SMEM(lon_width.shape, I32),
            vmem((1, block_cells.shape[0]), I32),
            vmem((1, block_owner.shape[0]), I32),
            vmem((1, channel_count.shape[0]), I32),
            vmem((1, hidden), F32),
            vmem((1, hidden), F32),
            vmem((1, channels), F32),
            vmem(grid, F32),
            vmem(grid, F32),
            vmem((recv_cols, channels), BF16),
            vmem((levels, hidden), BF16),
            vmem((hidden, hidden), BF16),
            vmem((hidden, channels), BF16),
            vmem(grid, F32),
            vmem(grid, F32),
            vmem((2, per_side, levels, width), F32),
            vmem((3, per_side, levels, width), F32),
            vmem((3, per_side, levels, width), F32),
            vmem((n_lat, 1, 128), F32),
            vmem((n_lat, BLOCK_COLS, channels), BF16),
            vmem((n_lat, BLOCK_COLS, channels), BF16),
            vmem(grid, F32),
            vmem((2 * levels, main + 2 * side), BF16),
            vmem((3 * levels, main), BF16),
            vmem((4 * levels, 3 * side), BF16),
            vmem((main + 2 * side, slots), BF16),
            vmem((main + 2 * side, slots), BF16),
            vmem((main, slots), BF16),
            vmem((3 * side, side), BF16),
            vmem((3 * side, side), BF16),
            vmem((levels, slots), F32),
            vmem((slots, levels), BF16),
            vmem((slots, hidden), BF16),
            vmem((slots, hidden), BF16),
            vmem((slots // min(BACK_PARTS, n_far), hidden), BF16),
            vmem((slots, hidden), BF16),
            vmem((slots, channels), F32),
            vmem((slots // min(BACK_PARTS, n_far), channels), BF16),
            vmem((hidden, levels), BF16),
            vmem((hidden, hidden), BF16),
            vmem((channels, hidden), BF16),
            vmem((slots, main + 2 * side), BF16),
            vmem(grid, F32),
            vmem(grid, BF16),
            vmem((2, levels, side), BF16),
            vmem(grid, BF16),
            vmem(grid, BF16),
            vmem((3, levels, side), BF16),
            vmem((3, levels, side), BF16),
            dma((14,)),
            dma((n_lat,)),
            dma((n_lat,)),
            dma((n_lat,)),
            dma((n_lat,)),
            dma((8,)),
            dma((8,)),
            dma((6 + 2 * CHUNKS,)),
            dma((6 + 2 * CHUNKS,)),
        ],
        compiler_params=pltpu.CompilerParams(
            collective_id=0, has_side_effects=True, vmem_limit_bytes=36 * 1024 * 1024
        ),
    )(
        *(
            pltpu.with_memory_space_constraint(value, pltpu.HBM)
            for value in (
                control,
                background,
                lon_width,
                block_cells.T,
                block_owner.T,
                channel_count.T,
                radiance.T,
                in_weight,
                in_bias.reshape(1, -1),
                mid_weight,
                mid_bias.reshape(1, -1),
                out_weight,
                out_bias.reshape(1, -1),
            )
        )
    )
    return control + adjoint


def solution(mesh):
    return jax.shard_map(
        functools.partial(shards, mesh.shape["lat"], mesh.shape["lon"]),
        mesh=mesh,
        in_specs=(
            P("lat", None, "lon"),
            P("lat", None, "lon"),
            P("lat"),
            P("lat", "lon"),
            P("lat", "lon"),
            P("lat", "lon"),
            P("lat", "lon"),
            P(),
            P(),
            P(),
            P(),
            P(),
            P(),
        ),
        out_specs=P("lat", None, "lon"),
        check_vma=False,
    )
```
